32 devices in a mesh: row: 4 (over z), col: 8 (over y, x, core).
Axes of the slice: x: 2, y: 2, z: 4, core: 2. Of those that a mesh axis runs over, the one named last changes fastest.
Arguments:
- latents: bfloat16 [112, 64, 512], P('row', 'col'), may hold values from -6 to 6
- w_conv: bfloat16 [3, 3, 512, 512], P(None, None, None, 'col'), may hold values from -0.09375 to 0.09375
- conv_bias: float32 [512], replicated, may hold values from -3 to 3
- w_qkv: bfloat16 [3, 512, 512], P(None, None, 'col')
- owners: int32 [4], replicated, may hold values from 0 to 15
Outputs:
- mixed: bfloat16 [112, 64, 512], P('row', 'col')
The draws below stay inside these ranges and needn't reach their ends.
All inputs are finite; a program needn't handle non-finite values.
Results may differ from the reference program's by a relative error of at most 0.0062.
Values may be sent and summed in bfloat16 or wider, within the bound.
A program may use at most 64 MiB of HBM per device.

```python
import jax
import jax.numpy as jnp
from jax import lax

C = 512
BR = 28
BC = 8
TILES = 4
TILE_DEV = 2
H = 112
W = 64
N_ROW = 4
N_COL = 8
DEVICES = 32


def draw_w_qkv(key, part):
    base = jax.random.normal(jax.random.fold_in(key, 11), (3, C, C), jnp.float32) * C ** (-0.5)
    whole = jnp.stack([base[0], 2.5 * base[1], 6.0 * base[2]], axis=0)
    return whole.astype(jnp.bfloat16)


def place_ends(result, rng, smallest, largest):
    dims = result.shape
    spot = [jax.random.randint(jax.random.fold_in(rng, axis), (), 0, dims[axis]) for axis in range(len(dims))]
    result = result.at[tuple(spot)].set(smallest)
    longest = dims.index(max(dims))
    spot[longest] = (spot[longest] + 1) % dims[longest]
    return result.at[tuple(spot)].set(largest)


def level_of(stream_key, dims, pieces, least, largest):
    def one(dim, blocks):
        steps = jax.random.uniform(jax.random.fold_in(jax.random.fold_in(stream_key, 6), dim), (blocks,), jnp.float32, least / len(pieces), largest / len(pieces))
        return jnp.repeat(jnp.exp(steps), dims[dim] // blocks).reshape((-1,) + (1,) * (len(dims) - dim - 1))

    factor_of = one(*pieces[0])
    for cut in pieces[1:]:
        factor_of = factor_of * one(*cut)
    return factor_of


def bell_draw(own_key, extent, scale, limit, shards=(), held_as=jnp.bfloat16):
    loudness = level_of(own_key, extent, shards, -0.22, 0.18) if shards else 1.0
    drawn = jax.random.normal(own_key, extent, jnp.float32) * scale * loudness
    return jnp.minimum(jnp.maximum(drawn, -limit), limit).astype(held_as)


def setup_inputs(seed: int = 0) -> dict:
    key_list = jax.random.split(jax.random.key(seed), 6)
    latents = bell_draw(key_list[0], (H, W, C), 1.0, 6.0, ((0, 4), (1, 8)))
    w_conv = bell_draw(key_list[1], (3, 3, C, C), (9 * C) ** -0.5, 0.09375, ((3, 8),))
    conv_bias = bell_draw(key_list[2], (C,), 0.5, 3.0, (), jnp.float32)
    w_qkv = draw_w_qkv(jax.random.fold_in(key_list[5], 71), 0)
    owners = place_ends(jax.random.randint(key_list[4], (TILES,), 0, DEVICES // TILE_DEV), jax.random.fold_in(key_list[4], 1), 0, (DEVICES // TILE_DEV) - 1).astype(jnp.int32)
    return dict(latents=latents, w_conv=w_conv, conv_bias=conv_bias, w_qkv=w_qkv, owners=owners)


def reference(latents, w_conv, conv_bias, w_qkv, owners):
    height, width, chans = latents.shape
    padded = jnp.pad(latents, ((1, 1), (1, 1), (0, 0)))
    conv = jnp.zeros((height * width, chans), jnp.float32)
    for shift_r in range(3):
        for shift_c in range(3):
            window = padded[shift_r:shift_r + height, shift_c:shift_c + width].reshape(-1, chans)
            conv = conv + jnp.dot(window, w_conv[shift_r, shift_c], preferred_element_type=jnp.float32)
    hidden = jax.nn.silu(conv + conv_bias[None, :]).astype(jnp.bfloat16)
    query = jnp.dot(hidden, w_qkv[0], preferred_element_type=jnp.float32).astype(jnp.bfloat16)
    key = jnp.dot(hidden, w_qkv[1], preferred_element_type=jnp.float32).astype(jnp.bfloat16)
    value = jnp.dot(hidden, w_qkv[2], preferred_element_type=jnp.float32).astype(jnp.bfloat16)

    def by_device(field):
        shaped = field.reshape(N_ROW, BR, N_COL, BC, chans)
        return jnp.transpose(shaped, (0, 2, 1, 3, 4)).reshape(N_ROW * N_COL, BR * BC, chans)

    picks = (TILE_DEV * owners[:, None] + jnp.arange(TILE_DEV, dtype=jnp.int32)[None, :]).reshape(-1).astype(jnp.int32)
    keys = by_device(key)[picks].reshape(-1, chans)
    values = by_device(value)[picks].reshape(-1, chans)
    scale = chans ** -0.5

    def one_row(rows):
        scores = jnp.dot(rows, keys.T, preferred_element_type=jnp.float32) * scale
        peak = jnp.max(scores, axis=1, keepdims=True)
        weights = jnp.exp(scores - peak)
        total = jnp.sum(weights, axis=1, keepdims=True)
        return jnp.dot(weights.astype(jnp.bfloat16), values, preferred_element_type=jnp.float32) / total

    attended = lax.map(one_row, query.reshape(height, width, chans))
    return (latents.astype(jnp.float32) + attended).astype(jnp.bfloat16)
```

```python
import functools

import jax
import jax.numpy as jnp
from jax import lax
from jax.experimental import pallas as pl
from jax.experimental.pallas import tpu as pltpu
from jax.sharding import PartitionSpec as P

TILES = 4
TILE_DEV = 2
CORES = 2
MESH = pl.DeviceIdType.MESH
VMEM_LIMIT = 56 * 1024 * 1024
NT = (((1,), (1,)), ((), ()))


def remote(src, dst, send, recv, target):
    return pltpu.make_async_remote_copy(
        src_ref=src, dst_ref=dst, send_sem=send, recv_sem=recv, device_id=target, device_id_type=MESH
    )


def chips_around(chip, n_chip):
    if n_chip == 4:
        beside = chip + 1 - 2 * lax.rem(chip, 2)
        across = lax.rem(chip + 2, n_chip)
        return [beside, across], lax.rem(beside + 2, n_chip)
    return [lax.rem(chip + i, n_chip) for i in range(1, n_chip)], None


def spread(row, col, n_col, src, place, send, recv, fsend, sends):
    chip, core = col // CORES, lax.rem(col, CORES)
    n_chip = n_col // CORES
    partner = chip * CORES + 1 - core
    near, far = chips_around(chip, n_chip)

    def go(source, target, send_sem, recv_sem, device):
        copy = remote(source, target, send_sem, recv_sem, (row, device))
        copy.start()
        sends.append(copy)

    def start(q):
        for i, other in enumerate(near if q % 2 == 0 else near[::-1]):
            go(src(q), place(q, col), send.at[q, i], recv.at[q, col], other * CORES + core)
        go(src(q), place(q, col), fsend.at[q, chip], recv.at[q, col], partner)

    def wait(q, who):
        remote(src(q), place(q, who), fsend.at[q, chip], recv.at[q, who], (row, partner)).wait_recv()

    def forward(q, origin):
        who = origin * CORES + core
        go(place(q, who), place(q, who), fsend.at[q, origin], recv.at[q, who], partner)

    def pass_near(q):
        order = near if q % 2 == 0 else near[::-1]
        for k, origin in enumerate(order):
            who = origin * CORES + core
            wait(q, who)
            if far is not None and k == 0:
                go(place(q, who), place(q, who), send.at[q, 2], recv.at[q, who], order[1] * CORES + core)
            forward(q, origin)

    def pass_far(q):
        if far is not None:
            wait(q, far * CORES + core)
            forward(q, far)

    def settle(q):
        for i in range(n_chip):
            wait(q, lax.rem(chip + i, n_chip) * CORES + 1 - core)

    return start, pass_near, pass_far, settle


def block_kernel(
    n_row, n_col, owners_ref, lat_ref, taps_ref, bias_ref, w_ref, out_ref,
    img, lat, taps, wide, hid, sel, up_in, up_out, dn_in, dn_out, tok, own, wbuf,
    lsem, isend, irecv, hsend, hrecv, csend, crecv,
    up_send, up_recv, dn_send, dn_recv, tsend, trecv, tfsend,
    asend, arecv, wsend, wrecv, wfsend,
):
    row, col = lax.axis_index("row"), lax.axis_index("col")
    chip, core = col // CORES, lax.rem(col, CORES)
    n_chip = n_col // CORES
    partner = chip * CORES + 1 - core
    near, far = chips_around(chip, n_chip)
    rows, cols, chans = lat_ref.shape
    half = rows // CORES
    group = hid.shape[2]
    count = half * cols
    slots = TILES * TILE_DEV
    has_up, has_down = row > 0, row < n_row - 1
    top = core == 0
    up_all, down_all = jnp.logical_and(has_up, top), jnp.logical_and(has_down, jnp.logical_not(top))

    barrier = pltpu.get_barrier_semaphore()

    def hello(target):
        pl.semaphore_signal(barrier, inc=1, device_id=target, device_id_type=MESH)

    for i in range(1, n_col):
        hello((row, lax.rem(col + i, n_col)))

    @pl.when(has_up)
    def _():
        hello((row - 1, col))

    @pl.when(has_down)
    def _():
        hello((row + 1, col))

    @pl.when(up_all)
    def _():
        for i in range(1, n_col):
            hello((row - 1, lax.rem(col + i, n_col)))

    @pl.when(down_all)
    def _():
        for i in range(1, n_col):
            hello((row + 1, lax.rem(col + i, n_col)))

    def piece(to_core):
        return lat_ref.at[pl.ds(0, half + 1)] if to_core == 0 else lat_ref.at[pl.ds(half - 1, half + 1)]

    def slot(who, to_core):
        return img.at[who, pl.ds(1 - to_core, half + 1)]

    local = [
        pltpu.make_async_copy(lat_ref, lat, lsem.at[0]),
        pltpu.make_async_copy(taps_ref, taps.at[:, :, core], lsem.at[1]),
        pltpu.make_async_copy(w_ref, wbuf.at[:, col], lsem.at[2]),
    ]
    for copy in local:
        copy.start()
    for to_core in range(CORES):

        @pl.when(core == to_core)
        def _():
            pltpu.make_async_copy(piece(to_core), slot(col, to_core), lsem.at[3]).start()

    @pl.when(jnp.logical_and(top, jnp.logical_not(has_up)))
    def _():
        for who in range(n_col):
            img[who, 0] = jnp.zeros((cols, chans), img.dtype)

    @pl.when(jnp.logical_and(jnp.logical_not(top), jnp.logical_not(has_down)))
    def _():
        for who in range(n_col):
            img[who, half + 1] = jnp.zeros((cols, chans), img.dtype)

    across_up = jnp.where(top, n_chip + 1, n_chip)
    across_down = jnp.where(top, n_chip, n_chip + 1)
    expect = n_col - 1 + jnp.where(has_up, across_up, 0) + jnp.where(has_down, across_down, 0)
    pl.semaphore_wait(barrier, expect)

    sends = []

    def go(copy):
        copy.start()
        sends.append(copy)

    def image(i, other, to_core, who):
        return remote(
            piece(to_core), slot(who, to_core), isend.at[i, to_core], irecv.at[who], (row, other * CORES + to_core)
        )

    if far is None:
        for i, other in enumerate(near):
            for to_core in range(CORES):
                go(image(i, other, to_core, col))
    else:
        first, second = jnp.where(top, near[0], near[1]), jnp.where(top, near[1], near[0])
        for i, other in enumerate((first, second)):
            for to_core in range(CORES):
                go(image(i, other, to_core, col))

    def to_partner(to_core):
        return remote(
            piece(to_core), slot(col, to_core), csend.at[0], irecv.at[col], (row, chip * CORES + to_core)
        )

    for to_core in range(CORES):

        @pl.when(core == 1 - to_core)
        def _():
            to_partner(to_core).start()

    taps_copy = remote(taps_ref, taps.at[:, :, core], csend.at[1], crecv, (row, partner))
    taps_copy.start()

    def edge(other, down):
        if down:
            return remote(
                lat_ref.at[rows - 1], img.at[col, 0], hsend.at[0, other], hrecv.at[col],
                (row + 1, other * CORES),
            )
        return remote(
            lat_ref.at[0], img.at[col, half + 1], hsend.at[1, other], hrecv.at[col],
            (row - 1, other * CORES + 1),
        )

    @pl.when(has_down)
    def _():
        for other in range(n_chip):
            edge(other, True).start()

    @pl.when(has_up)
    def _():
        for other in range(n_chip):
            edge(other, False).start()

    span = half + 1

    def strip_in(who):
        remote(
            lat_ref.at[pl.ds(0, span)], img.at[who, pl.ds(0, span)], csend.at[0], irecv.at[who], (row, partner)
        ).wait_recv()

    def edge_in(who):
        @pl.when(jnp.logical_or(up_all, down_all))
        def _():
            remote(lat_ref.at[0], img.at[who, 0], csend.at[0], hrecv.at[who], (row, partner)).wait_recv()

    def convolve(pair):
        total = None
        for tap in range(3):
            window = jnp.concatenate(
                [img[who, pl.ds(tap, half)].reshape(count, chans) for who in pair], axis=0
            )
            kernel = taps[tap].reshape(3 * group, chans)
            part = lax.dot_general(window, kernel, NT, preferred_element_type=jnp.float32)
            total = part if total is None else total + part
        for i, who in enumerate(pair):
            wide[who] = total[i * count:(i + 1) * count]

    w_start, w_near, w_far, w_settle = spread(
        row, col, n_col, lambda q: w_ref.at[q], lambda q, who: wbuf.at[q, who],
        wsend, wrecv, wfsend, sends,
    )

    local[1].wait()
    taps_copy.wait_recv()
    pltpu.make_async_copy(lat_ref.at[pl.ds(0, span)], img.at[col, pl.ds(0, span)], lsem.at[3]).wait()
    strip_in(partner)
    edge_in(col)
    edge_in(partner)
    if far is None:
        convolve((chip * CORES, chip * CORES + 1))
        for q in range(3):
            w_start(q)

        def other_chip(i, _):
            other = lax.rem(chip + i, n_chip)
            for who in (other * CORES, other * CORES + 1):
                strip_in(who)
                edge_in(who)
            convolve((other * CORES, other * CORES + 1))
            return 0

        lax.fori_loop(1, n_chip, other_chip, 0)
    else:

        def relay(k, who, target):
            for to_core in range(CORES):

                @pl.when(core == to_core)
                def _():
                    remote(
                        slot(who, to_core), slot(who, to_core), isend.at[2, k], irecv.at[who],
                        (row, target * CORES + to_core),
                    ).start()

        def relayed(k, who):
            remote(
                img.at[who, pl.ds(0, span)], img.at[who, pl.ds(0, span)], isend.at[2, k], irecv.at[who],
                (row, partner),
            ).wait_send()

        convolve((chip * CORES, chip * CORES + 1))
        early = (near[0] * CORES, near[1] * CORES + 1)
        late = (near[0] * CORES + 1, near[1] * CORES)
        last = (far * CORES, far * CORES + 1)
        strip_in(early[0])
        relay(0, early[0], near[1])
        strip_in(early[1])
        relay(1, early[1], near[0])
        for q in range(3):
            w_start(q)
        for who in early:
            edge_in(who)
        convolve(early)
        for pair in (late, last):
            for who in pair:
                strip_in(who)
                edge_in(who)
            convolve(pair)

    bias = None
    for k in range(n_chip):
        mine = jnp.where(chip == k, bias_ref[:, k * group:(k + 1) * group], 0.0)
        bias = mine if bias is None else bias + mine
    lane = lax.broadcasted_iota(jnp.int32, (half, cols, group), 1)

    def part_of(who, tap):
        return wide[who, :, pl.ds(tap * group, group)].reshape(half, cols, group)

    previous = jnp.zeros((half, cols, group), jnp.float32)
    after = pltpu.roll(part_of(0, 2), cols - 1, 1)
    for who in range(n_col):
        left = pltpu.roll(part_of(who, 0), 1, 1)
        right = after
        if who + 1 < n_col:
            after = pltpu.roll(part_of(who + 1, 2), cols - 1, 1)
        else:
            after = jnp.zeros((half, cols, group), jnp.float32)
        conv = part_of(who, 1) + jnp.where(lane == 0, previous, left) + jnp.where(lane == cols - 1, after, right)
        previous = left
        conv = (conv + bias.reshape(1, 1, group)).reshape(count, group)
        hid[who] = (conv * jax.nn.sigmoid(conv)).astype(hid.dtype)

    for tile in range(TILES):
        flat = TILE_DEV * owners_ref[tile]
        here = flat // n_col == row
        for member in range(TILE_DEV):
            block = hid[lax.rem(flat, n_col) + member]
            block = jnp.where(here, block, jnp.zeros_like(block))
            q = tile * TILE_DEV + member
            sel[q] = block
            up_out[q] = block
            dn_out[q] = block

    def up_copy(t):
        return remote(up_out.at[t], up_in.at[t], up_send.at[t], up_recv.at[t], (row + 1, col))

    def dn_copy(t):
        return remote(dn_out.at[t], dn_in.at[t], dn_send.at[t], dn_recv.at[t], (row - 1, col))

    @pl.when(jnp.logical_not(has_up))
    def _():
        for t in range(slots):
            up_copy(t).start()
            up_in[t] = jnp.zeros(up_in.shape[1:], up_in.dtype)

    @pl.when(jnp.logical_not(has_down))
    def _():
        for t in range(slots):
            dn_copy(t).start()
            dn_in[t] = jnp.zeros(dn_in.shape[1:], dn_in.dtype)

    for i in range(1, n_col):
        who = lax.rem(col + i, n_col)
        go(remote(hid.at[who], own.at[core, chip], asend.at[i], arecv.at[col], (row, who)))
    own[core, chip] = hid[col]

    def tok_at(q, who):
        return tok.at[who // CORES, q, lax.rem(who, CORES)]

    t_start, t_near, t_far, t_settle = spread(
        row, col, n_col, lambda q: tok_at(q, col), tok_at, tsend, trecv, tfsend, sends
    )
    lower = row < n_row // 2

    def upward(t, cond):
        @pl.when(jnp.logical_and(cond, has_up))
        def _():
            up_copy(t).wait_recv()

            @pl.when(has_down)
            def _():
                up_out[t] = sel[t] + up_in[t]
                up_copy(t).start()

    def downward(t, cond):
        @pl.when(jnp.logical_and(cond, has_down))
        def _():
            dn_copy(t).wait_recv()

            @pl.when(has_up)
            def _():
                dn_out[t] = sel[t] + dn_in[t]
                dn_copy(t).start()

    for q in range(3):
        w_near(q)
    for t in range(slots):
        for ahead in (0, 1) if t == 0 else (t + 1,):
            if ahead < slots:
                upward(ahead, lower)
                downward(ahead, jnp.logical_not(lower))
        downward(t, lower)
        upward(t, jnp.logical_not(lower))
        tok[chip, t, core] = sel[t] + up_in[t] + dn_in[t]
        t_start(t)

    for q in range(3):
        w_far(q)
    for q in range(slots):
        t_near(q)
    for i in range(1, n_col):
        who = lax.rem(col + i, n_col)
        remote(
            hid.at[0], own.at[lax.rem(who, CORES), who // CORES], asend.at[i], arecv.at[who], (row, partner)
        ).wait_recv()
    local[2].wait()
    for q in range(3):
        w_settle(q)

    mine = jnp.concatenate(
        [jnp.concatenate([own[c, k] for k in range(n_chip)], axis=1) for c in range(CORES)], axis=0
    )

    def weights(q):
        return wbuf[q].reshape(chans, chans)

    query = lax.dot_general(mine, weights(0), NT, preferred_element_type=jnp.float32).astype(jnp.bfloat16)
    query = jnp.dot(query, weights(1), preferred_element_type=jnp.float32)
    query = (query * chans ** (-0.5)).astype(jnp.bfloat16)

    peak = total = accum = None
    for t in range(TILES):
        for q in range(t * TILE_DEV, (t + 1) * TILE_DEV):
            t_far(q)
        for q in range(t * TILE_DEV, (t + 1) * TILE_DEV):
            t_settle(q)
        keys = jnp.concatenate(
            [
                tok[k, t * TILE_DEV:(t + 1) * TILE_DEV].reshape(TILE_DEV * CORES * count, group)
                for k in range(n_chip)
            ],
            axis=1,
        )
        score = lax.dot_general(query, keys, NT, preferred_element_type=jnp.float32)
        fresh = jnp.max(score, axis=1, keepdims=True)
        if t:
            fresh = jnp.maximum(fresh, peak)
            factor = jnp.exp(peak - fresh)
            total = total * factor
            accum = accum * factor
        peak = fresh
        weight = jnp.exp(score - peak)
        part = jnp.sum(weight, axis=1, keepdims=True)
        mixed = jnp.dot(weight.astype(jnp.bfloat16), keys, preferred_element_type=jnp.float32)
        total = part if t == 0 else total + part
        accum = mixed if t == 0 else accum + mixed
    context = (accum / total).astype(jnp.bfloat16)
    attended = lax.dot_general(context, weights(2), NT, preferred_element_type=jnp.float32)
    local[0].wait()
    out_ref[...] = (lat[...].astype(jnp.float32) + attended.reshape(rows, cols, chans)).astype(out_ref.dtype)

    for to_core in range(CORES):

        @pl.when(core == 1 - to_core)
        def _():
            to_partner(to_core).wait_send()

    taps_copy.wait_send()
    if far is not None:
        relayed(0, early[0])
        relayed(1, early[1])

    @pl.when(has_down)
    def _():
        for other in range(n_chip):
            edge(other, True).wait_send()
        for t in range(slots):
            up_copy(t).wait_send()

    @pl.when(has_up)
    def _():
        for other in range(n_chip):
            edge(other, False).wait_send()
        for t in range(slots):
            dn_copy(t).wait_send()

    for copy in sends:
        copy.wait_send()


def vmem():
    return pl.BlockSpec(memory_space=pltpu.VMEM)


def anywhere():
    return pl.BlockSpec(memory_space=pl.ANY)


def body(n_row, n_col, latents, w_conv, conv_bias, w_qkv, owners):
    rows, cols, chans = latents.shape
    width = w_conv.shape[3]
    n_chip = n_col // CORES
    group, half = width * CORES, rows // CORES
    count, slots = half * cols, TILES * TILE_DEV
    dma = pltpu.SemaphoreType.DMA
    bf16 = jnp.bfloat16
    line = pltpu.VMEM((slots, count, group), bf16)
    return pl.pallas_call(
        functools.partial(block_kernel, n_row, n_col),
        out_shape=jax.ShapeDtypeStruct((rows, cols, chans), bf16),
        in_specs=[pl.BlockSpec(memory_space=pltpu.SMEM), anywhere(), anywhere(), vmem(), anywhere()],
        out_specs=vmem(),
        scratch_shapes=[
            pltpu.VMEM((n_col, half + 2, cols, chans), bf16),
            pltpu.VMEM((rows, cols, chans), bf16),
            pltpu.VMEM((3, 3, CORES, width, chans), bf16),
            pltpu.VMEM((n_col, count, 3 * group), jnp.float32),
            pltpu.VMEM((n_col, count, group), bf16),
            line, line, line, line, line,
            pltpu.VMEM((n_chip, slots, CORES, count, group), bf16),
            pltpu.VMEM((CORES, n_chip, count, group), bf16),
            pltpu.VMEM((3, n_col, width, chans), bf16),
            dma((4,)), dma((max(n_chip - 1, 3), CORES)), dma((n_col,)),
            dma((2, n_chip)), dma((n_col,)), dma((2,)), dma,
            dma((slots,)), dma((slots,)), dma((slots,)), dma((slots,)),
            dma((slots, n_chip)), dma((slots, n_col)), dma((slots, n_chip)),
            dma((n_col,)), dma((n_col,)),
            dma((3, n_chip)), dma((3, n_col)), dma((3, n_chip)),
        ],
        compiler_params=pltpu.CompilerParams(
            collective_id=0, has_side_effects=True, vmem_limit_bytes=VMEM_LIMIT
        ),
    )(
        owners, latents, jnp.transpose(w_conv, (0, 1, 3, 2)), conv_bias.reshape(1, chans),
        jnp.transpose(w_qkv, (0, 2, 1)),
    )


def solution(mesh):
    placed = (P("row", "col", None), P(None, None, None, "col"), P(), P(None, None, "col"), P())
    return jax.shard_map(
        functools.partial(body, mesh.shape["row"], mesh.shape["col"]),
        mesh=mesh, in_specs=placed, out_specs=P("row", "col", None), check_vma=False,
    )
```

```python
import functools

import jax
import jax.numpy as jnp
from jax import lax
from jax.experimental import pallas as pl
from jax.experimental.pallas import tpu as pltpu
from jax.sharding import PartitionSpec as P

TILES = 4
TILE_DEV = 2
CORES = 2
MESH = pl.DeviceIdType.MESH
VMEM_LIMIT = 56 * 1024 * 1024
NT = (((1,), (1,)), ((), ()))


def remote(src, dst, send, recv, target):
    return pltpu.make_async_remote_copy(
        src_ref=src, dst_ref=dst, send_sem=send, recv_sem=recv, device_id=target, device_id_type=MESH
    )


def chips_around(chip, n_chip):
    if n_chip == 4:
        beside = chip + 1 - 2 * lax.rem(chip, 2)
        across = lax.rem(chip + 2, n_chip)
        return [beside, across], lax.rem(beside + 2, n_chip)
    return [lax.rem(chip + i, n_chip) for i in range(1, n_chip)], None


def spread(row, col, n_col, src, place, send, recv, fsend, sends, direct=lambda q: False):
    chip, core = col // CORES, lax.rem(col, CORES)
    n_chip = n_col // CORES
    partner = chip * CORES + 1 - core
    near, far = chips_around(chip, n_chip)

    def go(source, target, send_sem, recv_sem, device):
        copy = remote(source, target, send_sem, recv_sem, (row, device))
        copy.start()
        sends.append(copy)

    def start(q):
        for i, other in enumerate(near if q % 2 == 0 else near[::-1]):
            go(src(q), place(q, col), send.at[q, i], recv.at[q, col], other * CORES + core)
        if far is not None and direct(q):
            go(src(q), place(q, col), send.at[q, 2], recv.at[q, col], far * CORES + core)
        go(src(q), place(q, col), fsend.at[q, chip], recv.at[q, col], partner)

    def wait(q, who):
        remote(src(q), place(q, who), fsend.at[q, chip], recv.at[q, who], (row, partner)).wait_recv()

    def forward(q, origin):
        who = origin * CORES + core
        go(place(q, who), place(q, who), fsend.at[q, origin], recv.at[q, who], partner)

    def pass_near(q):
        order = near if q % 2 == 0 else near[::-1]
        for k, origin in enumerate(order):
            who = origin * CORES + core
            wait(q, who)
            if far is not None and k == 0 and not direct(q):
                go(place(q, who), place(q, who), send.at[q, 2], recv.at[q, who], order[1] * CORES + core)
            forward(q, origin)

    def pass_far(q):
        if far is not None:
            wait(q, far * CORES + core)
            forward(q, far)

    def settle(q):
        for i in range(n_chip):
            wait(q, lax.rem(chip + i, n_chip) * CORES + 1 - core)

    return start, pass_near, pass_far, settle


def block_kernel(
    n_row, n_col, cuts, owners_hbm, lat_ref, taps_ref, bias_hbm, w_ref, out_ref,
    owners_ref, bias_ref, img, lat, edges, taps, wide, hid,
    sel0, up_in0, up_out0, dn_in0, dn_out0, tok0,
    sel1, up_in1, up_out1, dn_in1, dn_out1, tok1, own, wbuf,
    lsem, isend, irecv, zsend, zrecv, hsend, hrecv, csend, crecv,
    up_send, up_recv, dn_send, dn_recv, tsend, trecv, tfsend,
    asend, arecv, wsend, wrecv, wfsend,
):
    row, col = lax.axis_index("row"), lax.axis_index("col")
    chip, core = col // CORES, lax.rem(col, CORES)
    n_chip = n_col // CORES
    partner = chip * CORES + 1 - core
    near, far = chips_around(chip, n_chip)
    rows, cols, chans = lat_ref.shape
    half = rows // CORES
    group = hid.shape[2]
    count = half * cols
    slots = 2 * TILES
    has_up, has_down = row > 0, row < n_row - 1
    top = core == 0

    barrier = pltpu.get_barrier_semaphore()

    def hello(target):
        pl.semaphore_signal(barrier, inc=1, device_id=target, device_id_type=MESH)

    @pl.when(has_up)
    def _():
        hello((row - 1, col))

    @pl.when(has_down)
    def _():
        hello((row + 1, col))

    for other in near:
        for c in range(CORES):
            hello((row, other * CORES + c))
    hello((row, partner))

    first_rows = cuts[0] + 2
    own_rows = ((1, first_rows, half + 2), (0, first_rows, half + 1))

    def piece(p, to_core, who=None):
        lo, hi = own_rows[to_core][p], own_rows[to_core][p + 1]
        if who is None:
            return lat_ref.at[pl.ds(lo - 1 + to_core * half, hi - lo)]
        return img.at[who, pl.ds(lo, hi - lo)]

    local = [
        pltpu.make_async_copy(taps_ref, taps.at[:, :, core], lsem.at[0]),
        pltpu.make_async_copy(lat_ref, lat, lsem.at[1]),
        pltpu.make_async_copy(w_ref, wbuf.at[:, col], lsem.at[2]),
        pltpu.make_async_copy(bias_hbm, bias_ref, lsem.at[3]),
        pltpu.make_async_copy(owners_hbm, owners_ref, lsem.at[4]),
    ]

    def edge_row(to_core):
        return 0 if to_core == 0 else half + 1

    @pl.when(jnp.logical_and(top, jnp.logical_not(has_up)))
    def _():
        for who in range(n_col):
            img[who, edge_row(0)] = jnp.zeros((cols, chans), img.dtype)

    @pl.when(jnp.logical_and(jnp.logical_not(top), jnp.logical_not(has_down)))
    def _():
        for who in range(n_col):
            img[who, edge_row(1)] = jnp.zeros((cols, chans), img.dtype)

    pl.semaphore_wait(barrier, CORES * len(near) + 1 + has_up.astype(jnp.int32) + has_down.astype(jnp.int32))

    sends = []

    def go(copy):
        copy.start()
        sends.append(copy)

    def z_copy(to_core):
        if to_core == 0:
            return remote(lat_ref.at[rows - 1], edges.at[0], zsend.at[0], zrecv.at[0], (row + 1, col))
        return remote(lat_ref.at[0], edges.at[1], zsend.at[1], zrecv.at[1], (row - 1, col))

    @pl.when(has_down)
    def _():
        z_copy(0).start()

    @pl.when(has_up)
    def _():
        z_copy(1).start()

    def image(p, i, other):
        for to_core in range(CORES):
            go(remote(
                piece(p, to_core), piece(p, to_core, col), isend.at[p, i, to_core], irecv.at[p, col],
                (row, other * CORES + to_core),
            ))

    if far is None:
        order = near
    else:
        order = [jnp.where(top, near[0], near[1]), jnp.where(top, near[1], near[0])]
    for i, other in enumerate(order):
        image(0, i, other)

    taps_copy = remote(taps_ref, taps.at[:, :, core], csend.at[2], crecv, (row, partner))
    taps_copy.start()
    local[0].start()

    def to_partner(p, to_core):
        return remote(
            piece(p, to_core), piece(p, to_core, col), csend.at[p], irecv.at[p, col], (row, chip * CORES + to_core)
        )

    def to_self(p, to_core):
        return pltpu.make_async_copy(piece(p, to_core), piece(p, to_core, col), lsem.at[5 + p])

    for to_core in range(CORES):

        @pl.when(core == to_core)
        def _():
            for p in range(2):
                to_self(p, to_core).start()

        @pl.when(core == 1 - to_core)
        def _():
            for p in range(2):
                to_partner(p, to_core).start()

    for copy in local[1:]:
        copy.start()

    def edge_place(to_core, who):
        return img.at[who, edge_row(to_core)]

    def edge_out(to_core, i):
        if i < len(near):
            target = near[i] * CORES + to_core
        else:
            target = partner
        return remote(
            edges.at[to_core], edge_place(to_core, col), hsend.at[to_core, i], hrecv.at[col], (row, target)
        )

    def edge_self(to_core):
        return pltpu.make_async_copy(edges.at[to_core], edge_place(to_core, col), lsem.at[7])

    def on_edges(act):
        for to_core in range(CORES):

            @pl.when(has_up if to_core == 0 else has_down)
            def _():
                act(to_core)

    def edge_spread(to_core):
        z_copy(to_core).wait_recv()
        for i in range(len(near)):
            edge_out(to_core, i).start()

        @pl.when(core == to_core)
        def _():
            edge_self(to_core).start()

        @pl.when(core != to_core)
        def _():
            edge_out(to_core, len(near)).start()

    on_edges(edge_spread)

    def on_my_edge(act):
        for to_core in range(CORES):

            @pl.when(jnp.logical_and(core == to_core, has_up if to_core == 0 else has_down))
            def _():
                act(to_core)

    def edge_in(who):
        on_my_edge(lambda to_core: remote(
            edges.at[to_core], edge_place(to_core, who), csend.at[0], hrecv.at[who], (row, partner)
        ).wait_recv())

    def strip_in(p, who):
        for to_core in range(CORES):

            @pl.when(core == to_core)
            def _():
                remote(
                    piece(p, to_core, who), piece(p, to_core, who), csend.at[0], irecv.at[p, who], (row, partner)
                ).wait_recv()

    def relay(p, k, who, target):
        for to_core in range(CORES):

            @pl.when(core == to_core)
            def _():
                remote(
                    piece(p, to_core, who), piece(p, to_core, who), isend.at[p, 2, k], irecv.at[p, who],
                    (row, target * CORES + to_core),
                ).start()

    def relayed(p, k, who):
        for to_core in range(CORES):

            @pl.when(core == to_core)
            def _():
                remote(
                    piece(p, to_core, who), piece(p, to_core, who), isend.at[p, 2, k], irecv.at[p, who],
                    (row, partner),
                ).wait_send()

    def edge_relay(k, who, target):
        return lambda to_core: remote(
            edge_place(to_core, who), edge_place(to_core, who), csend.at[3 + k], hrecv.at[who],
            (row, target * CORES + to_core),
        )

    spans = (cuts[0], half - cuts[0])
    starts = (0, cuts[0])

    def convolve(p, group_of):
        size = spans[p] * cols
        total = None
        for tap in range(3):
            window = jnp.concatenate(
                [img[who, pl.ds(starts[p] + tap, spans[p])].reshape(size, chans) for who in group_of], axis=0
            )
            kernel = taps[tap].reshape(3 * group, chans)
            part = lax.dot_general(window, kernel, NT, preferred_element_type=jnp.float32)
            total = part if total is None else total + part
        for i, who in enumerate(group_of):
            wide[who, pl.ds(starts[p], spans[p])] = total[i * size:(i + 1) * size].reshape(
                spans[p], cols, 3 * group
            )

    def finish(p):
        bias = None
        for k in range(n_chip):
            mine = jnp.where(chip == k, bias_ref[:, k * group:(k + 1) * group], 0.0)
            bias = mine if bias is None else bias + mine
        bias = bias.reshape(1, 1, group)
        shape = (spans[p], cols, group)
        at = lax.broadcasted_iota(jnp.int32, shape, 1)

        def part_of(who, tap):
            return wide[who, pl.ds(starts[p], spans[p]), :, pl.ds(tap * group, group)]

        previous = jnp.zeros(shape, jnp.float32)
        after = pltpu.roll(part_of(0, 2), cols - 1, 1)
        for who in range(n_col):
            left = pltpu.roll(part_of(who, 0), 1, 1)
            right = after
            if who + 1 < n_col:
                after = pltpu.roll(part_of(who + 1, 2), cols - 1, 1)
            else:
                after = jnp.zeros(shape, jnp.float32)
            conv = part_of(who, 1) + jnp.where(at == 0, previous, left) + jnp.where(at == cols - 1, after, right)
            previous = left
            conv = (conv + bias).reshape(spans[p] * cols, group)
            hid[who, pl.ds(starts[p] * cols, spans[p] * cols)] = (conv * jax.nn.sigmoid(conv)).astype(hid.dtype)

    sels, up_ins, up_outs = (sel0, sel1), (up_in0, up_in1), (up_out0, up_out1)
    dn_ins, dn_outs, toks = (dn_in0, dn_in1), (dn_out0, dn_out1), (tok0, tok1)

    def at(pair, q):
        return pair[q // TILES].at[q % TILES]

    def up_copy(q):
        return remote(at(up_outs, q), at(up_ins, q), up_send.at[q], up_recv.at[q], (row + 1, col))

    def dn_copy(q):
        return remote(at(dn_outs, q), at(dn_ins, q), dn_send.at[q], dn_recv.at[q], (row - 1, col))

    def select(p):
        for tile in range(TILES):
            q = p * TILES + tile
            flat = TILE_DEV * owners_ref[tile]
            here = flat // n_col == row
            for member in range(TILE_DEV):
                block = hid[lax.rem(flat, n_col) + member, pl.ds(starts[p] * cols, spans[p] * cols)]
                block = jnp.where(here, block, jnp.zeros_like(block))
                for kept in (sels, up_outs, dn_outs):
                    at(kept, q)[member] = block

            @pl.when(jnp.logical_not(has_up))
            def _():
                up_copy(q).start()
                at(up_ins, q)[...] = jnp.zeros(up_ins[p].shape[1:], hid.dtype)

            @pl.when(jnp.logical_not(has_down))
            def _():
                dn_copy(q).start()
                at(dn_ins, q)[...] = jnp.zeros(dn_ins[p].shape[1:], hid.dtype)

    w_start, w_near, w_far, w_settle = spread(
        row, col, n_col, lambda q: w_ref.at[q], lambda q, who: wbuf.at[q, who],
        wsend, wrecv, wfsend, sends,
    )

    def mine_in(p):
        for to_core in range(CORES):

            @pl.when(core == to_core)
            def _():
                to_self(p, to_core).wait()

        strip_in(p, partner)

    def edges_in(group_of):
        for who in group_of:
            if who is col:
                on_my_edge(lambda to_core: edge_self(to_core).wait())
            else:
                edge_in(who)

    pair = (col, partner)
    if far is None:
        local[0].wait()
        taps_copy.wait_recv()
        edges_in(pair)
        for i, other in enumerate(order):
            image(1, i, other)
        for q in range(3):
            w_start(q)
        for p in range(2):
            mine_in(p)
            convolve(p, pair)

            def other_chip(i, _):
                other = lax.rem(chip + i, n_chip)
                for who in (other * CORES, other * CORES + 1):
                    strip_in(p, who)
                    if p == 0:
                        edge_in(who)
                convolve(p, (other * CORES, other * CORES + 1))
                return 0

            lax.fori_loop(1, n_chip, other_chip, 0)
            if p == 0:
                for copy in local[3:]:
                    copy.wait()
            finish(p)
            select(p)
    else:
        early = (near[0] * CORES, near[1] * CORES + 1)
        late = (near[0] * CORES + 1, near[1] * CORES)
        last = (far * CORES, far * CORES + 1)
        image(1, 0, order[0])
        for k in range(2):
            strip_in(0, early[k])
            relay(0, k, early[k], near[1 - k])
        image(1, 1, order[1])
        local[0].wait()
        taps_copy.wait_recv()
        mine_in(0)
        for k in range(2):
            edge_in(early[k])
            on_my_edge(lambda to_core: edge_relay(k, early[k], near[1 - k])(to_core).start())
        for k in range(2):
            strip_in(1, early[k])
            relay(1, k, early[k], near[1 - k])
        for q in range(3):
            w_start(q)
        edges_in(pair)
        convolve(0, pair + early)
        for who in late:
            strip_in(0, who)
            edge_in(who)
        convolve(0, late)
        for who in last:
            strip_in(0, who)
            edge_in(who)
        convolve(0, last)
        for copy in local[3:]:
            copy.wait()
        finish(0)
        select(0)
        mine_in(1)
        convolve(1, pair + early)
        for who in late:
            strip_in(1, who)
        convolve(1, late)
        for who in last:
            strip_in(1, who)
        convolve(1, last)
        finish(1)
        select(1)

    for i in range(1, n_col):
        who = lax.rem(col + i, n_col)
        go(remote(hid.at[who], own.at[core, chip], asend.at[i], arecv.at[col], (row, who)))
    own[core, chip] = hid[col]

    def tok_at(q, who):
        return toks[q // TILES].at[who // CORES, q % TILES, lax.rem(who, CORES)]

    t_start, t_near, t_far, t_settle = spread(
        row, col, n_col, lambda q: tok_at(q, col), tok_at, tsend, trecv, tfsend, sends,
        direct=lambda q: q >= TILES,
    )
    lower = row < n_row // 2

    def upward(q, cond):
        @pl.when(jnp.logical_and(cond, has_up))
        def _():
            up_copy(q).wait_recv()

            @pl.when(has_down)
            def _():
                at(up_outs, q)[...] = at(sels, q)[...] + at(up_ins, q)[...]
                up_copy(q).start()

    def downward(q, cond):
        @pl.when(jnp.logical_and(cond, has_down))
        def _():
            dn_copy(q).wait_recv()

            @pl.when(has_up)
            def _():
                at(dn_outs, q)[...] = at(sels, q)[...] + at(dn_ins, q)[...]
                dn_copy(q).start()

    w_near(0)
    for q in range(slots):
        for ahead in range(TILES) if q == 0 else (q + TILES - 1,):
            if ahead < slots:
                upward(ahead, lower)
                downward(ahead, jnp.logical_not(lower))
        if q == 0:
            w_near(1)
            w_near(2)
        downward(q, lower)
        upward(q, jnp.logical_not(lower))
        tok_at(q, col)[...] = at(sels, q)[...] + at(up_ins, q)[...] + at(dn_ins, q)[...]
        t_start(q)
        if q == TILES - 1:
            for k in range(3):
                w_far(k)
        if q >= TILES:
            t_near(q - TILES)

    for i in range(1, n_col):
        who = lax.rem(col + i, n_col)
        remote(
            hid.at[0], own.at[lax.rem(who, CORES), who // CORES], asend.at[i], arecv.at[who], (row, partner)
        ).wait_recv()
    local[2].wait()
    for q in range(3):
        w_settle(q)

    mine = jnp.concatenate(
        [jnp.concatenate([own[c, k] for k in range(n_chip)], axis=1) for c in range(CORES)], axis=0
    )

    def weights(q):
        return wbuf[q].reshape(chans, chans)

    query = lax.dot_general(mine, weights(0), NT, preferred_element_type=jnp.float32).astype(jnp.bfloat16)
    query = jnp.dot(query, weights(1), preferred_element_type=jnp.float32)
    query = (query * chans ** (-0.5)).astype(jnp.bfloat16)

    for q in range(TILES):
        t_far(q)

    def keys_of(q):
        found = toks[q // TILES]
        size = CORES * TILE_DEV * found.shape[4]
        return jnp.concatenate([found[k, q % TILES].reshape(size, group) for k in range(n_chip)], axis=1)

    peak = total = accum = None
    for t in range(0, slots, 2):
        if t == TILES:
            for q in range(TILES, slots):
                t_near(q)
            for q in range(TILES, slots):
                t_far(q)
        for q in (t, t + 1):
            t_settle(q)
        keys = jnp.concatenate([keys_of(t), keys_of(t + 1)], axis=0)
        score = lax.dot_general(query, keys, NT, preferred_element_type=jnp.float32)
        fresh = jnp.max(score, axis=1, keepdims=True)
        if t:
            fresh = jnp.maximum(fresh, peak)
            factor = jnp.exp(peak - fresh)
            total = total * factor
            accum = accum * factor
        peak = fresh
        weight = jnp.exp(score - peak)
        part = jnp.sum(weight, axis=1, keepdims=True)
        mixed = jnp.dot(weight.astype(jnp.bfloat16), keys, preferred_element_type=jnp.float32)
        total = part if t == 0 else total + part
        accum = mixed if t == 0 else accum + mixed
    context = (accum / total).astype(jnp.bfloat16)
    attended = lax.dot_general(context, weights(2), NT, preferred_element_type=jnp.float32)
    local[1].wait()
    out_ref[...] = (lat[...].astype(jnp.float32) + attended.reshape(rows, cols, chans)).astype(out_ref.dtype)

    for to_core in range(CORES):

        @pl.when(core == 1 - to_core)
        def _():
            for p in range(2):
                to_partner(p, to_core).wait_send()

    taps_copy.wait_send()

    def edge_sent(to_core):
        for i in range(len(near)):
            edge_out(to_core, i).wait_send()

        @pl.when(core != to_core)
        def _():
            edge_out(to_core, len(near)).wait_send()

    on_edges(edge_sent)
    if far is not None:
        for p in range(2):
            for k in range(2):
                relayed(p, k, early[k])
        for k in range(2):
            on_my_edge(lambda to_core: edge_relay(k, early[k], near[1 - k])(to_core).wait_send())

    @pl.when(has_down)
    def _():
        z_copy(0).wait_send()
        for q in range(slots):
            up_copy(q).wait_send()

    @pl.when(has_up)
    def _():
        z_copy(1).wait_send()
        for q in range(slots):
            dn_copy(q).wait_send()

    for copy in sends:
        copy.wait_send()


def vmem():
    return pl.BlockSpec(memory_space=pltpu.VMEM)


def anywhere():
    return pl.BlockSpec(memory_space=pl.ANY)


def body(n_row, n_col, latents, w_conv, conv_bias, w_qkv, owners):
    rows, cols, chans = latents.shape
    width = w_conv.shape[3]
    n_chip = n_col // CORES
    group, half = width * CORES, rows // CORES
    first = (half // 4 + 1) * 2
    count, slots = half * cols, 2 * TILES
    dma = pltpu.SemaphoreType.DMA
    bf16 = jnp.bfloat16
    parts = []
    for span in (first, half - first):
        line = pltpu.VMEM((TILES, TILE_DEV, span * cols, group), bf16)
        parts += [line] * 5 + [pltpu.VMEM((n_chip, TILES, CORES, TILE_DEV, span * cols, group), bf16)]
    return pl.pallas_call(
        functools.partial(block_kernel, n_row, n_col, (first,)),
        out_shape=jax.ShapeDtypeStruct((rows, cols, chans), bf16),
        in_specs=[anywhere()] * 5,
        out_specs=vmem(),
        scratch_shapes=[
            pltpu.SMEM((TILES,), jnp.int32),
            pltpu.VMEM((1, chans), jnp.float32),
            pltpu.VMEM((n_col, half + 2, cols, chans), bf16),
            pltpu.VMEM((rows, cols, chans), bf16),
            pltpu.VMEM((2, cols, chans), bf16),
            pltpu.VMEM((3, 3, CORES, width, chans), bf16),
            pltpu.VMEM((n_col, half, cols, 3 * group), jnp.float32),
            pltpu.VMEM((n_col, count, group), bf16),
            *parts,
            pltpu.VMEM((CORES, n_chip, count, group), bf16),
            pltpu.VMEM((3, n_col, width, chans), bf16),
            dma((8,)), dma((2, max(n_chip - 1, 3), CORES)), dma((2, n_col)),
            dma((2,)), dma((2,)), dma((2, n_chip)), dma((n_col,)), dma((5,)), dma,
            dma((slots,)), dma((slots,)), dma((slots,)), dma((slots,)),
            dma((slots, max(n_chip, 3))), dma((slots, n_col)), dma((slots, n_chip)),
            dma((n_col,)), dma((n_col,)),
            dma((3, n_chip)), dma((3, n_col)), dma((3, n_chip)),
        ],
        compiler_params=pltpu.CompilerParams(
            collective_id=0, has_side_effects=True, vmem_limit_bytes=VMEM_LIMIT
        ),
    )(
        owners, latents, jnp.transpose(w_conv, (0, 1, 3, 2)), conv_bias.reshape(1, chans),
        jnp.transpose(w_qkv, (0, 2, 1)),
    )


def solution(mesh):
    placed = (P("row", "col", None), P(None, None, None, "col"), P(), P(None, None, "col"), P())
    return jax.shard_map(
        functools.partial(body, mesh.shape["row"], mesh.shape["col"]),
        mesh=mesh, in_specs=placed, out_specs=P("row", "col", None), check_vma=False,
    )
```

```python
import functools

import jax
import jax.numpy as jnp
from jax import lax
from jax.experimental import pallas as pl
from jax.experimental.pallas import tpu as pltpu
from jax.sharding import PartitionSpec as P

TILES = 4
TILE_DEV = 2
CORES = 2
MESH = pl.DeviceIdType.MESH
VMEM_LIMIT = 56 * 1024 * 1024
NT = (((1,), (1,)), ((), ()))


def remote(src, dst, send, recv, target):
    return pltpu.make_async_remote_copy(
        src_ref=src, dst_ref=dst, send_sem=send, recv_sem=recv, device_id=target, device_id_type=MESH
    )


def chips_around(chip, n_chip):
    if n_chip == 4:
        beside = chip + 1 - 2 * lax.rem(chip, 2)
        across = lax.rem(chip + 2, n_chip)
        return [beside, across], lax.rem(beside + 2, n_chip)
    return [lax.rem(chip + i, n_chip) for i in range(1, n_chip)], None


def spread(row, col, n_col, src, place, send, recv, fsend, sends):
    chip, core = col // CORES, lax.rem(col, CORES)
    n_chip = n_col // CORES
    partner = chip * CORES + 1 - core
    near, far = chips_around(chip, n_chip)

    def go(source, target, send_sem, recv_sem, device):
        copy = remote(source, target, send_sem, recv_sem, (row, device))
        copy.start()
        sends.append(copy)

    def start(q):
        for i, other in enumerate(near if q % 2 == 0 else near[::-1]):
            go(src(q), place(q, col), send.at[q, i], recv.at[q, col], other * CORES + core)
        go(src(q), place(q, col), fsend.at[q, chip], recv.at[q, col], partner)

    def wait(q, who):
        remote(src(q), place(q, who), fsend.at[q, chip], recv.at[q, who], (row, partner)).wait_recv()

    def forward(q, origin):
        who = origin * CORES + core
        go(place(q, who), place(q, who), fsend.at[q, origin], recv.at[q, who], partner)

    def pass_near(q):
        order = near if q % 2 == 0 else near[::-1]
        for k, origin in enumerate(order):
            who = origin * CORES + core
            wait(q, who)
            if far is not None and k == 0:
                go(place(q, who), place(q, who), send.at[q, 2], recv.at[q, who], order[1] * CORES + core)
            forward(q, origin)

    def pass_far(q):
        if far is not None:
            wait(q, far * CORES + core)
            forward(q, far)

    def settle(q):
        for i in range(n_chip):
            wait(q, lax.rem(chip + i, n_chip) * CORES + 1 - core)

    return start, pass_near, pass_far, settle


def block_kernel(
    n_row, n_col, spans, owners_hbm, lat_ref, taps_ref, bias_hbm, w_ref, out_ref,
    owners_ref, bias_ref, img, lat, edges, taps, wide, hid,
    sels, up_ins, up_outs, dn_ins, dn_outs, toks, own, wbuf, queries, share_out, share_in,
    lsem, isend, irecv, zsend, zrecv, hsend, hrecv, csend, crecv,
    up_send, up_recv, dn_send, dn_recv, tsend, trecv, qsend, qrecv, ssend, srecv,
    asend, arecv, wsend, wrecv, wfsend,
):
    row, col = lax.axis_index("row"), lax.axis_index("col")
    chip, core = col // CORES, lax.rem(col, CORES)
    n_chip = n_col // CORES
    partner = chip * CORES + 1 - core
    near, far = chips_around(chip, n_chip)
    rows, cols, chans = lat_ref.shape
    half = rows // CORES
    group = hid.shape[2]
    count = half * cols
    parts = len(spans)
    starts = [sum(spans[:p]) for p in range(parts)]
    slots = parts * TILES
    has_up, has_down = row > 0, row < n_row - 1
    top = core == 0

    barrier = pltpu.get_barrier_semaphore()

    def hello(target):
        pl.semaphore_signal(barrier, inc=1, device_id=target, device_id_type=MESH)

    @pl.when(has_up)
    def _():
        hello((row - 1, col))

    @pl.when(has_down)
    def _():
        hello((row + 1, col))

    for other in near:
        for c in range(CORES):
            hello((row, other * CORES + c))
    hello((row, partner))

    inner = tuple(start + 2 for start in starts[1:])
    own_rows = ((1, *inner, half + 2), (0, *inner, half + 1))

    def piece(p, to_core, who=None):
        lo, hi = own_rows[to_core][p], own_rows[to_core][p + 1]
        if who is None:
            return lat_ref.at[pl.ds(lo - 1 + to_core * half, hi - lo)]
        return img.at[who, pl.ds(lo, hi - lo)]

    local = [
        pltpu.make_async_copy(taps_ref, taps.at[:, :, core], lsem.at[0]),
        pltpu.make_async_copy(lat_ref, lat, lsem.at[1]),
        pltpu.make_async_copy(w_ref, wbuf.at[:, col], lsem.at[2]),
        pltpu.make_async_copy(bias_hbm, bias_ref, lsem.at[3]),
        pltpu.make_async_copy(owners_hbm, owners_ref, lsem.at[4]),
    ]

    def edge_row(to_core):
        return 0 if to_core == 0 else half + 1

    @pl.when(jnp.logical_and(top, jnp.logical_not(has_up)))
    def _():
        for who in range(n_col):
            img[who, edge_row(0)] = jnp.zeros((cols, chans), img.dtype)

    @pl.when(jnp.logical_and(jnp.logical_not(top), jnp.logical_not(has_down)))
    def _():
        for who in range(n_col):
            img[who, edge_row(1)] = jnp.zeros((cols, chans), img.dtype)

    pl.semaphore_wait(barrier, CORES * len(near) + 1 + has_up.astype(jnp.int32) + has_down.astype(jnp.int32))

    sends = []

    def go(copy):
        copy.start()
        sends.append(copy)

    def z_copy(to_core):
        if to_core == 0:
            return remote(lat_ref.at[rows - 1], edges.at[0], zsend.at[0], zrecv.at[0], (row + 1, col))
        return remote(lat_ref.at[0], edges.at[1], zsend.at[1], zrecv.at[1], (row - 1, col))

    @pl.when(has_down)
    def _():
        z_copy(0).start()

    @pl.when(has_up)
    def _():
        z_copy(1).start()

    def image(p, i, other):
        for to_core in range(CORES):
            go(remote(
                piece(p, to_core), piece(p, to_core, col), isend.at[p, i, to_core], irecv.at[p, col],
                (row, other * CORES + to_core),
            ))

    if far is None:
        order = near
    else:
        order = [jnp.where(top, near[0], near[1]), jnp.where(top, near[1], near[0])]
    for i, other in enumerate(order):
        image(0, i, other)

    taps_copy = remote(taps_ref, taps.at[:, :, core], csend.at[0], crecv, (row, partner))
    taps_copy.start()
    local[0].start()

    def to_partner(p, to_core):
        return remote(
            piece(p, to_core), piece(p, to_core, col), csend.at[3 + p], irecv.at[p, col], (row, chip * CORES + to_core)
        )

    def to_self(p, to_core):
        return pltpu.make_async_copy(piece(p, to_core), piece(p, to_core, col), lsem.at[6 + p])

    for to_core in range(CORES):

        @pl.when(core == to_core)
        def _():
            for p in range(parts):
                to_self(p, to_core).start()

        @pl.when(core == 1 - to_core)
        def _():
            for p in range(parts):
                to_partner(p, to_core).start()

    for copy in local[1:]:
        copy.start()

    def edge_place(to_core, who):
        return img.at[who, edge_row(to_core)]

    def edge_out(to_core, i):
        if i < len(near):
            target = near[i] * CORES + to_core
        else:
            target = partner
        return remote(
            edges.at[to_core], edge_place(to_core, col), hsend.at[to_core, i], hrecv.at[col], (row, target)
        )

    def edge_self(to_core):
        return pltpu.make_async_copy(edges.at[to_core], edge_place(to_core, col), lsem.at[5])

    def on_edges(act):
        for to_core in range(CORES):

            @pl.when(has_up if to_core == 0 else has_down)
            def _():
                act(to_core)

    def edge_spread(to_core):
        z_copy(to_core).wait_recv()
        for i in range(len(near)):
            edge_out(to_core, i).start()

        @pl.when(core == to_core)
        def _():
            edge_self(to_core).start()

        @pl.when(core != to_core)
        def _():
            edge_out(to_core, len(near)).start()

    on_edges(edge_spread)

    def on_my_edge(act):
        for to_core in range(CORES):

            @pl.when(jnp.logical_and(core == to_core, has_up if to_core == 0 else has_down))
            def _():
                act(to_core)

    def edge_in(who):
        on_my_edge(lambda to_core: remote(
            edges.at[to_core], edge_place(to_core, who), csend.at[0], hrecv.at[who], (row, partner)
        ).wait_recv())

    def strip_in(p, who):
        for to_core in range(CORES):

            @pl.when(core == to_core)
            def _():
                remote(
                    piece(p, to_core, who), piece(p, to_core, who), csend.at[0], irecv.at[p, who], (row, partner)
                ).wait_recv()

    def relay(p, k, who, target):
        for to_core in range(CORES):

            @pl.when(core == to_core)
            def _():
                remote(
                    piece(p, to_core, who), piece(p, to_core, who), isend.at[p, 2, k], irecv.at[p, who],
                    (row, target * CORES + to_core),
                ).start()

    def relayed(p, k, who):
        for to_core in range(CORES):

            @pl.when(core == to_core)
            def _():
                remote(
                    piece(p, to_core, who), piece(p, to_core, who), isend.at[p, 2, k], irecv.at[p, who],
                    (row, partner),
                ).wait_send()

    def edge_relay(k, who, target):
        return lambda to_core: remote(
            edge_place(to_core, who), edge_place(to_core, who), csend.at[1 + k], hrecv.at[who],
            (row, target * CORES + to_core),
        )

    def convolve(p, group_of):
        size = spans[p] * cols
        total = None
        for tap in range(3):
            window = jnp.concatenate(
                [img[who, pl.ds(starts[p] + tap, spans[p])].reshape(size, chans) for who in group_of], axis=0
            )
            kernel = taps[tap].reshape(3 * group, chans)
            part = lax.dot_general(window, kernel, NT, preferred_element_type=jnp.float32)
            total = part if total is None else total + part
        for i, who in enumerate(group_of):
            wide[who, pl.ds(starts[p], spans[p])] = total[i * size:(i + 1) * size].reshape(
                spans[p], cols, 3 * group
            )

    def finish(p):
        bias = None
        for k in range(n_chip):
            mine = jnp.where(chip == k, bias_ref[:, k * group:(k + 1) * group], 0.0)
            bias = mine if bias is None else bias + mine
        bias = bias.reshape(1, 1, group)
        shape = (spans[p], cols, group)
        at = lax.broadcasted_iota(jnp.int32, shape, 1)

        def part_of(who, tap):
            return wide[who, pl.ds(starts[p], spans[p]), :, pl.ds(tap * group, group)]

        previous = jnp.zeros(shape, jnp.float32)
        after = pltpu.roll(part_of(0, 2), cols - 1, 1)
        for who in range(n_col):
            left = pltpu.roll(part_of(who, 0), 1, 1)
            right = after
            if who + 1 < n_col:
                after = pltpu.roll(part_of(who + 1, 2), cols - 1, 1)
            else:
                after = jnp.zeros(shape, jnp.float32)
            conv = part_of(who, 1) + jnp.where(at == 0, previous, left) + jnp.where(at == cols - 1, after, right)
            previous = left
            conv = (conv + bias).reshape(spans[p] * cols, group)
            hid[who, pl.ds(starts[p] * cols, spans[p] * cols)] = (conv * jax.nn.sigmoid(conv)).astype(hid.dtype)

    def at(pair, q):
        return pair[q // TILES].at[q % TILES]

    def up_copy(q):
        return remote(at(up_outs, q), at(up_ins, q), up_send.at[q], up_recv.at[q], (row + 1, col))

    def dn_copy(q):
        return remote(at(dn_outs, q), at(dn_ins, q), dn_send.at[q], dn_recv.at[q], (row - 1, col))

    def select(p):
        for tile in range(TILES):
            q = p * TILES + tile
            flat = TILE_DEV * owners_ref[tile]
            here = flat // n_col == row
            for member in range(TILE_DEV):
                block = hid[lax.rem(flat, n_col) + member, pl.ds(starts[p] * cols, spans[p] * cols)]
                block = jnp.where(here, block, jnp.zeros_like(block))
                for kept in (sels, up_outs, dn_outs):
                    at(kept, q)[member] = block

            @pl.when(jnp.logical_not(has_up))
            def _():
                up_copy(q).start()
                at(up_ins, q)[...] = jnp.zeros(up_ins[p].shape[1:], hid.dtype)

            @pl.when(jnp.logical_not(has_down))
            def _():
                dn_copy(q).start()
                at(dn_ins, q)[...] = jnp.zeros(dn_ins[p].shape[1:], hid.dtype)

    w_start, w_near, w_far, w_settle = spread(
        row, col, n_col, lambda q: w_ref.at[q], lambda q, who: wbuf.at[q, who],
        wsend, wrecv, wfsend, sends,
    )

    def mine_in(p):
        for to_core in range(CORES):

            @pl.when(core == to_core)
            def _():
                to_self(p, to_core).wait()

        strip_in(p, partner)

    def edges_in(group_of):
        for who in group_of:
            if who is col:
                on_my_edge(lambda to_core: edge_self(to_core).wait())
            else:
                edge_in(who)

    lower = row < n_row // 2

    def upward(q, cond):
        @pl.when(jnp.logical_and(cond, has_up))
        def _():
            up_copy(q).wait_recv()

            @pl.when(has_down)
            def _():
                at(up_outs, q)[...] = at(sels, q)[...] + at(up_ins, q)[...]
                up_copy(q).start()

    def downward(q, cond):
        @pl.when(jnp.logical_and(cond, has_down))
        def _():
            dn_copy(q).wait_recv()

            @pl.when(has_up)
            def _():
                at(dn_outs, q)[...] = at(sels, q)[...] + at(dn_ins, q)[...]
                dn_copy(q).start()

    def nearer(q):
        upward(q, lower)
        downward(q, jnp.logical_not(lower))

    def farther(q):
        downward(q, lower)
        upward(q, jnp.logical_not(lower))

    pair = (col, partner)
    if far is None:
        local[0].wait()
        taps_copy.wait_recv()
        edges_in(pair)
        for p in range(1, parts):
            for i, other in enumerate(order):
                image(p, i, other)
        for q in range(3):
            w_start(q)
        for p in range(parts):
            mine_in(p)
            convolve(p, pair)

            def other_chip(i, _):
                other = lax.rem(chip + i, n_chip)
                for who in (other * CORES, other * CORES + 1):
                    strip_in(p, who)
                    if p == 0:
                        edge_in(who)
                convolve(p, (other * CORES, other * CORES + 1))
                return 0

            lax.fori_loop(1, n_chip, other_chip, 0)
            if p == 0:
                for copy in local[3:]:
                    copy.wait()
            finish(p)
            select(p)
            if p == parts - 2:
                for q in range(TILES):
                    nearer(q)
    else:
        early = (near[0] * CORES, near[1] * CORES + 1)
        late = (near[0] * CORES + 1, near[1] * CORES)
        last = (far * CORES, far * CORES + 1)

        def relay_early(p):
            for k in range(2):
                strip_in(p, early[k])
                relay(p, k, early[k], near[1 - k])
                if p == 0:
                    edge_in(early[k])
                    on_my_edge(lambda to_core: edge_relay(k, early[k], near[1 - k])(to_core).start())

        for p in range(parts):
            if p + 1 < parts:
                image(p + 1, 0, order[0])
            if p < parts - 1:
                relay_early(p)
            if p + 1 < parts:
                image(p + 1, 1, order[1])
        local[0].wait()
        taps_copy.wait_recv()
        edges_in(pair)
        for p in range(parts):
            mine_in(p)
            convolve(p, pair + early)
            if p == parts - 2:
                relay_early(parts - 1)
                for q in range(3):
                    w_start(q)
            for who in late + last:
                strip_in(p, who)
                if p == 0:
                    edge_in(who)
            convolve(p, late + last)
            if p == 0:
                for copy in local[3:]:
                    copy.wait()
            finish(p)
            select(p)

    for i in range(1, n_col):
        who = lax.rem(col + i, n_col)
        go(remote(hid.at[who], own.at[core, chip], asend.at[i], arecv.at[col], (row, who)))
    own[core, chip] = hid[col]

    others = near if far is None else near + [far]

    def tok_at(q, of_chip):
        return toks[q // TILES].at[of_chip, q % TILES]

    def t_start(q):
        for i, other in enumerate(others):
            go(remote(
                tok_at(q, chip), tok_at(q, chip), tsend.at[q, i], trecv.at[q, chip], (row, other * CORES + core)
            ))

    def t_wait(q):
        for other in others:
            remote(
                tok_at(q, chip), tok_at(q, other), tsend.at[q, 0], trecv.at[q, other], (row, partner)
            ).wait_recv()

    w_near(0)
    for q in range(TILES):
        nearer(q)
    for q in range(slots):
        if q + TILES < slots:
            nearer(q + TILES)
        farther(q)
        tok_at(q, chip)[...] = at(sels, q)[...] + at(up_ins, q)[...] + at(dn_ins, q)[...]
        t_start(q)
        if q < 2:
            w_near(q + 1)

    for i in range(1, n_col):
        who = lax.rem(col + i, n_col)
        remote(
            hid.at[0], own.at[lax.rem(who, CORES), who // CORES], asend.at[i], arecv.at[who], (row, partner)
        ).wait_recv()
    local[2].wait()
    for q in range(3):
        w_far(q)
    for q in range(3):
        w_settle(q)

    mine = jnp.concatenate(
        [jnp.concatenate([own[c, k] for k in range(n_chip)], axis=1) for c in range(CORES)], axis=0
    )

    def weights(q):
        return wbuf[q].reshape(chans, chans)

    query = lax.dot_general(mine, weights(0), NT, preferred_element_type=jnp.float32).astype(jnp.bfloat16)
    query = jnp.dot(query, weights(1), preferred_element_type=jnp.float32)
    queries[0] = (query * chans ** (-0.5)).astype(jnp.bfloat16)
    query_copy = remote(queries.at[0], queries.at[1], qsend, qrecv, (row, partner))
    query_copy.start()
    query_copy.wait_recv()

    def keys_of(q):
        found = toks[q // TILES]
        size = TILE_DEV * found.shape[3]
        return jnp.concatenate([found[k, q % TILES].reshape(size, group) for k in range(n_chip)], axis=1)

    def attend(query, keys, state):
        score = lax.dot_general(query, keys, NT, preferred_element_type=jnp.float32)
        fresh = jnp.max(score, axis=1, keepdims=True)
        if state is not None:
            fresh = jnp.maximum(fresh, state[0])
        weight = jnp.exp(score - fresh)
        total = jnp.sum(weight, axis=1, keepdims=True)
        accum = jnp.dot(weight.astype(jnp.bfloat16), keys, preferred_element_type=jnp.float32)
        if state is not None:
            factor = jnp.exp(state[0] - fresh)
            total = total + state[1] * factor
            accum = accum + state[2] * factor
        return fresh, total, accum

    steps = [range(t, t + TILES) for t in range(0, slots - TILES, TILES)]
    steps += [range(t, t + TILES // 2) for t in (slots - TILES, slots - TILES // 2)]
    states = [None, None]
    for t, step in enumerate(steps):
        for q in step:
            t_wait(q)
        keys = jnp.concatenate([keys_of(q) for q in step], axis=0)
        states[1] = attend(queries[1], keys, states[1])
        if t == len(steps) - 1:
            peak, total, accum = states[1]
            share_out[:, :chans] = accum
            share_out[:, chans:chans + 128] = jnp.broadcast_to(peak, (rows * cols, 128))
            share_out[:, chans + 128:] = jnp.broadcast_to(total, (rows * cols, 128))
            share_copy = remote(share_out, share_in, ssend, srecv, (row, partner))
            share_copy.start()
        states[0] = attend(queries[0], keys, states[0])
    peak, total, accum = states[0]
    share_copy.wait_recv()
    its_peak, its_total = share_in[:, chans:chans + 1], share_in[:, chans + 128:chans + 129]
    fresh = jnp.maximum(peak, its_peak)
    mine, its = jnp.exp(peak - fresh), jnp.exp(its_peak - fresh)
    total = total * mine + its_total * its
    accum = accum * mine + share_in[:, :chans] * its
    context = (accum / total).astype(jnp.bfloat16)
    attended = lax.dot_general(context, weights(2), NT, preferred_element_type=jnp.float32)
    local[1].wait()
    out_ref[...] = (lat[...].astype(jnp.float32) + attended.reshape(rows, cols, chans)).astype(out_ref.dtype)

    for to_core in range(CORES):

        @pl.when(core == 1 - to_core)
        def _():
            for p in range(parts):
                to_partner(p, to_core).wait_send()

    taps_copy.wait_send()
    query_copy.wait_send()
    share_copy.wait_send()

    def edge_sent(to_core):
        for i in range(len(near)):
            edge_out(to_core, i).wait_send()

        @pl.when(core != to_core)
        def _():
            edge_out(to_core, len(near)).wait_send()

    on_edges(edge_sent)
    if far is not None:
        for p in range(parts):
            for k in range(2):
                relayed(p, k, early[k])
        for k in range(2):
            on_my_edge(lambda to_core: edge_relay(k, early[k], near[1 - k])(to_core).wait_send())

    @pl.when(has_down)
    def _():
        z_copy(0).wait_send()
        for q in range(slots):
            up_copy(q).wait_send()

    @pl.when(has_up)
    def _():
        z_copy(1).wait_send()
        for q in range(slots):
            dn_copy(q).wait_send()

    for copy in sends:
        copy.wait_send()


def vmem():
    return pl.BlockSpec(memory_space=pltpu.VMEM)


def anywhere():
    return pl.BlockSpec(memory_space=pl.ANY)


def body(n_row, n_col, latents, w_conv, conv_bias, w_qkv, owners):
    rows, cols, chans = latents.shape
    width = w_conv.shape[3]
    n_chip = n_col // CORES
    group, half = width * CORES, rows // CORES
    first = half // 4 * 2 + 2
    spans = (first, half - first)
    count, slots, parts = half * cols, len(spans) * TILES, len(spans)
    dma = pltpu.SemaphoreType.DMA
    bf16 = jnp.bfloat16
    line = tuple(pltpu.VMEM((TILES, TILE_DEV, span * cols, group), bf16) for span in spans)
    tokens = tuple(pltpu.VMEM((n_chip, TILES, TILE_DEV, span * cols, group), bf16) for span in spans)
    return pl.pallas_call(
        functools.partial(block_kernel, n_row, n_col, spans),
        out_shape=pltpu.VMEM((rows, cols, chans), bf16),
        in_specs=[anywhere()] * 5,
        out_specs=vmem(),
        scratch_shapes=[
            pltpu.SMEM((TILES,), jnp.int32),
            pltpu.VMEM((1, chans), jnp.float32),
            pltpu.VMEM((n_col, half + 2, cols, chans), bf16),
            pltpu.VMEM((rows, cols, chans), bf16),
            pltpu.VMEM((2, cols, chans), bf16),
            pltpu.VMEM((3, 3, CORES, width, chans), bf16),
            pltpu.VMEM((n_col, half, cols, 3 * group), jnp.float32),
            pltpu.VMEM((n_col, count, group), bf16),
            line, line, line, line, line, tokens,
            pltpu.VMEM((CORES, n_chip, count, group), bf16),
            pltpu.VMEM((3, n_col, width, chans), bf16),
            pltpu.VMEM((CORES, rows * cols, chans), bf16),
            pltpu.VMEM((rows * cols, chans + 256), jnp.float32),
            pltpu.VMEM((rows * cols, chans + 256), jnp.float32),
            dma((6 + parts,)), dma((parts, max(n_chip - 1, 3), CORES)), dma((parts, n_col)),
            dma((2,)), dma((2,)), dma((2, n_chip)), dma((n_col,)), dma((3 + parts,)), dma,
            dma((slots,)), dma((slots,)), dma((slots,)), dma((slots,)),
            dma((slots, n_chip)), dma((slots, n_chip)), dma, dma, dma, dma,
            dma((n_col,)), dma((n_col,)),
            dma((3, n_chip)), dma((3, n_col)), dma((3, n_chip)),
        ],
        compiler_params=pltpu.CompilerParams(
            collective_id=0, has_side_effects=True, vmem_limit_bytes=VMEM_LIMIT
        ),
    )(
        owners, latents, jnp.transpose(w_conv, (0, 1, 3, 2)), conv_bias.reshape(1, chans),
        jnp.transpose(w_qkv, (0, 2, 1)),
    )


def solution(mesh):
    placed = (P("row", "col", None), P(None, None, None, "col"), P(), P(None, None, "col"), P())
    return jax.shard_map(
        functools.partial(body, mesh.shape["row"], mesh.shape["col"]),
        mesh=mesh, in_specs=placed, out_specs=P("row", "col", None), check_vma=False,
    )
```

```python
import functools

import jax
import jax.numpy as jnp
from jax import lax
from jax.experimental import pallas as pl
from jax.experimental.pallas import tpu as pltpu
from jax.sharding import PartitionSpec as P

TILES = 4
TILE_DEV = 2
CORES = 2
MESH = pl.DeviceIdType.MESH
VMEM_LIMIT = 56 * 1024 * 1024
NT = (((1,), (1,)), ((), ()))


def remote(src, dst, send, recv, target):
    return pltpu.make_async_remote_copy(
        src_ref=src, dst_ref=dst, send_sem=send, recv_sem=recv, device_id=target, device_id_type=MESH
    )


def chips_around(chip, n_chip):
    if n_chip == 4:
        beside = chip + 1 - 2 * lax.rem(chip, 2)
        across = lax.rem(chip + 2, n_chip)
        return [beside, across], lax.rem(beside + 2, n_chip)
    return [lax.rem(chip + i, n_chip) for i in range(1, n_chip)], None


def spread(row, col, n_col, src, place, send, recv, fsend, sends):
    chip, core = col // CORES, lax.rem(col, CORES)
    n_chip = n_col // CORES
    partner = chip * CORES + 1 - core
    near, far = chips_around(chip, n_chip)

    def go(source, target, send_sem, recv_sem, device):
        copy = remote(source, target, send_sem, recv_sem, (row, device))
        copy.start()
        sends.append(copy)

    def start(q):
        for i, other in enumerate(near if q % 2 == 0 else near[::-1]):
            go(src(q), place(q, col), send.at[q, i], recv.at[q, col], other * CORES + core)
        go(src(q), place(q, col), fsend.at[q, chip], recv.at[q, col], partner)

    def wait(q, who):
        remote(src(q), place(q, who), fsend.at[q, chip], recv.at[q, who], (row, partner)).wait_recv()

    def forward(q, origin):
        who = origin * CORES + core
        go(place(q, who), place(q, who), fsend.at[q, origin], recv.at[q, who], partner)

    def pass_near(q):
        order = near if q % 2 == 0 else near[::-1]
        for k, origin in enumerate(order):
            who = origin * CORES + core
            wait(q, who)
            if far is not None and k == 0:
                go(place(q, who), place(q, who), send.at[q, 2], recv.at[q, who], order[1] * CORES + core)
            forward(q, origin)

    def pass_far(q):
        if far is not None:
            wait(q, far * CORES + core)
            forward(q, far)

    def settle(q):
        for i in range(n_chip):
            wait(q, lax.rem(chip + i, n_chip) * CORES + 1 - core)

    return start, pass_near, pass_far, settle


def block_kernel(
    n_row, n_col, spans, owners_hbm, lat_ref, taps_ref, bias_hbm, w_ref, out_ref,
    owners_ref, bias_ref, img, lat, edges, taps, wide, hid,
    sels, up_ins, up_outs, dn_ins, dn_outs, toks, own, wbuf, queries, share_out, share_in,
    lsem, isend, irecv, zsend, zrecv, hsend, hrecv, csend, crecv,
    up_send, up_recv, dn_send, dn_recv, tsend, trecv, qsend, qrecv, ssend, srecv,
    asend, arecv, wsend, wrecv, wfsend,
):
    row, col = lax.axis_index("row"), lax.axis_index("col")
    chip, core = col // CORES, lax.rem(col, CORES)
    n_chip = n_col // CORES
    partner = chip * CORES + 1 - core
    near, far = chips_around(chip, n_chip)
    rows, cols, chans = lat_ref.shape
    half = rows // CORES
    group = hid.shape[2]
    count = half * cols
    parts = len(spans)
    starts = [sum(spans[:p]) for p in range(parts)]
    slots = parts * TILES
    has_up, has_down = row > 0, row < n_row - 1
    top = core == 0

    barrier = pltpu.get_barrier_semaphore()

    def hello(target):
        pl.semaphore_signal(barrier, inc=1, device_id=target, device_id_type=MESH)

    @pl.when(has_up)
    def _():
        hello((row - 1, col))

    @pl.when(has_down)
    def _():
        hello((row + 1, col))

    for other in near:
        for c in range(CORES):
            hello((row, other * CORES + c))
    hello((row, partner))

    inner = tuple(start + 2 for start in starts[1:])
    own_rows = ((1, *inner, half + 2), (0, *inner, half + 1))

    def piece(p, to_core, who=None):
        lo, hi = own_rows[to_core][p], own_rows[to_core][p + 1]
        if who is None:
            return lat_ref.at[pl.ds(lo - 1 + to_core * half, hi - lo)]
        return img.at[who, pl.ds(lo, hi - lo)]

    local = [
        pltpu.make_async_copy(taps_ref, taps.at[:, :, core], lsem.at[0]),
        pltpu.make_async_copy(lat_ref, lat, lsem.at[1]),
        pltpu.make_async_copy(w_ref, wbuf.at[:, col], lsem.at[2]),
        pltpu.make_async_copy(bias_hbm, bias_ref, lsem.at[3]),
        pltpu.make_async_copy(owners_hbm, owners_ref, lsem.at[4]),
    ]

    def edge_row(to_core):
        return 0 if to_core == 0 else half + 1

    @pl.when(jnp.logical_and(top, jnp.logical_not(has_up)))
    def _():
        for who in range(n_col):
            img[who, edge_row(0)] = jnp.zeros((cols, chans), img.dtype)

    @pl.when(jnp.logical_and(jnp.logical_not(top), jnp.logical_not(has_down)))
    def _():
        for who in range(n_col):
            img[who, edge_row(1)] = jnp.zeros((cols, chans), img.dtype)

    pl.semaphore_wait(barrier, CORES * len(near) + 1 + has_up.astype(jnp.int32) + has_down.astype(jnp.int32))

    sends = []

    def go(copy):
        copy.start()
        sends.append(copy)

    def z_copy(to_core):
        if to_core == 0:
            return remote(lat_ref.at[rows - 1], edges.at[0], zsend.at[0], zrecv.at[0], (row + 1, col))
        return remote(lat_ref.at[0], edges.at[1], zsend.at[1], zrecv.at[1], (row - 1, col))

    @pl.when(has_down)
    def _():
        z_copy(0).start()

    @pl.when(has_up)
    def _():
        z_copy(1).start()

    def image(p, i, other):
        for to_core in range(CORES):
            go(remote(
                piece(p, to_core), piece(p, to_core, col), isend.at[p, i, to_core], irecv.at[p, col],
                (row, other * CORES + to_core),
            ))

    if far is None:
        order = near
    else:
        order = [jnp.where(top, near[0], near[1]), jnp.where(top, near[1], near[0])]
    for i, other in enumerate(order):
        image(0, i, other)

    taps_copy = remote(taps_ref, taps.at[:, :, core], csend.at[0], crecv, (row, partner))
    taps_copy.start()
    local[0].start()

    def to_partner(p, to_core):
        return remote(
            piece(p, to_core), piece(p, to_core, col), csend.at[3 + p], irecv.at[p, col], (row, chip * CORES + to_core)
        )

    def to_self(p, to_core):
        return pltpu.make_async_copy(piece(p, to_core), piece(p, to_core, col), lsem.at[6 + p])

    for to_core in range(CORES):

        @pl.when(core == to_core)
        def _():
            for p in range(parts):
                to_self(p, to_core).start()

        @pl.when(core == 1 - to_core)
        def _():
            for p in range(parts):
                to_partner(p, to_core).start()

    for copy in local[1:]:
        copy.start()

    def edge_place(to_core, who):
        return img.at[who, edge_row(to_core)]

    def edge_out(to_core, i):
        if i < len(near):
            target = near[i] * CORES + to_core
        else:
            target = partner
        return remote(
            edges.at[to_core], edge_place(to_core, col), hsend.at[to_core, i], hrecv.at[col], (row, target)
        )

    def edge_self(to_core):
        return pltpu.make_async_copy(edges.at[to_core], edge_place(to_core, col), lsem.at[5])

    def on_edges(act):
        for to_core in range(CORES):

            @pl.when(has_up if to_core == 0 else has_down)
            def _():
                act(to_core)

    def edge_spread(to_core):
        z_copy(to_core).wait_recv()
        for i in range(len(near)):
            edge_out(to_core, i).start()

        @pl.when(core == to_core)
        def _():
            edge_self(to_core).start()

        @pl.when(core != to_core)
        def _():
            edge_out(to_core, len(near)).start()

    on_edges(edge_spread)

    def on_my_edge(act):
        for to_core in range(CORES):

            @pl.when(jnp.logical_and(core == to_core, has_up if to_core == 0 else has_down))
            def _():
                act(to_core)

    def edge_in(who):
        on_my_edge(lambda to_core: remote(
            edges.at[to_core], edge_place(to_core, who), csend.at[0], hrecv.at[who], (row, partner)
        ).wait_recv())

    def strip_in(p, who):
        for to_core in range(CORES):

            @pl.when(core == to_core)
            def _():
                remote(
                    piece(p, to_core, who), piece(p, to_core, who), csend.at[0], irecv.at[p, who], (row, partner)
                ).wait_recv()

    def relay(p, k, who, target):
        for to_core in range(CORES):

            @pl.when(core == to_core)
            def _():
                remote(
                    piece(p, to_core, who), piece(p, to_core, who), isend.at[p, 2, k], irecv.at[p, who],
                    (row, target * CORES + to_core),
                ).start()

    def relayed(p, k, who):
        for to_core in range(CORES):

            @pl.when(core == to_core)
            def _():
                remote(
                    piece(p, to_core, who), piece(p, to_core, who), isend.at[p, 2, k], irecv.at[p, who],
                    (row, partner),
                ).wait_send()

    def edge_relay(k, who, target):
        return lambda to_core: remote(
            edge_place(to_core, who), edge_place(to_core, who), csend.at[1 + k], hrecv.at[who],
            (row, target * CORES + to_core),
        )

    def convolve(p, group_of):
        size = spans[p] * cols
        total = None
        for tap in range(3):
            window = jnp.concatenate(
                [img[who, pl.ds(starts[p] + tap, spans[p])].reshape(size, chans) for who in group_of], axis=0
            )
            kernel = taps[tap].reshape(3 * group, chans)
            part = lax.dot_general(window, kernel, NT, preferred_element_type=jnp.float32)
            total = part if total is None else total + part
        for i, who in enumerate(group_of):
            wide[who, pl.ds(starts[p], spans[p])] = total[i * size:(i + 1) * size].reshape(
                spans[p], cols, 3 * group
            )

    def finish(p):
        bias = None
        for k in range(n_chip):
            mine = jnp.where(chip == k, bias_ref[:, k * group:(k + 1) * group], 0.0)
            bias = mine if bias is None else bias + mine
        bias = bias.reshape(1, 1, group)
        shape = (spans[p], cols, group)
        at = lax.broadcasted_iota(jnp.int32, shape, 1)

        def part_of(who, tap):
            return wide[who, pl.ds(starts[p], spans[p]), :, pl.ds(tap * group, group)]

        previous = jnp.zeros(shape, jnp.float32)
        after = pltpu.roll(part_of(0, 2), cols - 1, 1)
        for who in range(n_col):
            left = pltpu.roll(part_of(who, 0), 1, 1)
            right = after
            if who + 1 < n_col:
                after = pltpu.roll(part_of(who + 1, 2), cols - 1, 1)
            else:
                after = jnp.zeros(shape, jnp.float32)
            conv = part_of(who, 1) + jnp.where(at == 0, previous, left) + jnp.where(at == cols - 1, after, right)
            previous = left
            conv = (conv + bias).reshape(spans[p] * cols, group)
            hid[who, pl.ds(starts[p] * cols, spans[p] * cols)] = (conv * jax.nn.sigmoid(conv)).astype(hid.dtype)

    def at(pair, q):
        return pair[q // TILES].at[q % TILES]

    def up_copy(q):
        return remote(at(up_outs, q), at(up_ins, q), up_send.at[q], up_recv.at[q], (row + 1, col))

    def dn_copy(q):
        return remote(at(dn_outs, q), at(dn_ins, q), dn_send.at[q], dn_recv.at[q], (row - 1, col))

    def select(p):
        for tile in range(TILES):
            q = p * TILES + tile
            flat = TILE_DEV * owners_ref[tile]
            here = flat // n_col == row
            for member in range(TILE_DEV):
                block = hid[lax.rem(flat, n_col) + member, pl.ds(starts[p] * cols, spans[p] * cols)]
                block = jnp.where(here, block, jnp.zeros_like(block))
                for kept in (sels, up_outs, dn_outs):
                    at(kept, q)[member] = block

            @pl.when(jnp.logical_not(has_up))
            def _():
                up_copy(q).start()
                at(up_ins, q)[...] = jnp.zeros(up_ins[p].shape[1:], hid.dtype)

            @pl.when(jnp.logical_not(has_down))
            def _():
                dn_copy(q).start()
                at(dn_ins, q)[...] = jnp.zeros(dn_ins[p].shape[1:], hid.dtype)

    w_start, w_near, w_far, w_settle = spread(
        row, col, n_col, lambda q: w_ref.at[q], lambda q, who: wbuf.at[q, who],
        wsend, wrecv, wfsend, sends,
    )

    def mine_in(p):
        for to_core in range(CORES):

            @pl.when(core == to_core)
            def _():
                to_self(p, to_core).wait()

        strip_in(p, partner)

    def edges_in(group_of):
        for who in group_of:
            if who is col:
                on_my_edge(lambda to_core: edge_self(to_core).wait())
            else:
                edge_in(who)

    lower = row < n_row // 2

    def upward(q, cond):
        @pl.when(jnp.logical_and(cond, has_up))
        def _():
            up_copy(q).wait_recv()

            @pl.when(has_down)
            def _():
                at(up_outs, q)[...] = at(sels, q)[...] + at(up_ins, q)[...]
                up_copy(q).start()

    def downward(q, cond):
        @pl.when(jnp.logical_and(cond, has_down))
        def _():
            dn_copy(q).wait_recv()

            @pl.when(has_up)
            def _():
                at(dn_outs, q)[...] = at(sels, q)[...] + at(dn_ins, q)[...]
                dn_copy(q).start()

    def nearer(q):
        upward(q, lower)
        downward(q, jnp.logical_not(lower))

    def farther(q):
        downward(q, lower)
        upward(q, jnp.logical_not(lower))

    pair = (col, partner)
    if far is None:
        local[0].wait()
        taps_copy.wait_recv()
        edges_in(pair)
        for p in range(1, parts):
            for i, other in enumerate(order):
                image(p, i, other)
        for q in range(3):
            w_start(q)
        for p in range(parts):
            mine_in(p)
            convolve(p, pair)

            def other_chip(i, _):
                other = lax.rem(chip + i, n_chip)
                for who in (other * CORES, other * CORES + 1):
                    strip_in(p, who)
                    if p == 0:
                        edge_in(who)
                convolve(p, (other * CORES, other * CORES + 1))
                return 0

            lax.fori_loop(1, n_chip, other_chip, 0)
            if p == 0:
                for copy in local[3:]:
                    copy.wait()
            finish(p)
            select(p)
            if p == parts - 2:
                for q in range(TILES):
                    nearer(q)
    else:
        early = (near[0] * CORES, near[1] * CORES + 1)
        late = (near[0] * CORES + 1, near[1] * CORES)
        last = (far * CORES, far * CORES + 1)

        def relay_early(p):
            for k in range(2):
                strip_in(p, early[k])
                relay(p, k, early[k], near[1 - k])
                if p == 0:
                    edge_in(early[k])
                    on_my_edge(lambda to_core: edge_relay(k, early[k], near[1 - k])(to_core).start())

        for p in range(parts):
            if p + 1 < parts:
                image(p + 1, 0, order[0])
            if p < parts - 1:
                relay_early(p)
            if p + 1 < parts:
                image(p + 1, 1, order[1])
        local[0].wait()
        taps_copy.wait_recv()
        edges_in(pair)
        for p in range(parts):
            mine_in(p)
            convolve(p, pair + early)
            if p == parts - 2:
                relay_early(parts - 1)
                for q in range(3):
                    w_start(q)
            for group_of in (late, last):
                for who in group_of:
                    strip_in(p, who)
                    if p == 0:
                        edge_in(who)
                convolve(p, group_of)
            if p == 0:
                for copy in local[3:]:
                    copy.wait()
            if p == parts - 1:
                nearer(0)
                nearer(1)
            finish(p)
            select(p)

    for i in range(1, n_col):
        who = lax.rem(col + i, n_col)
        go(remote(hid.at[who], own.at[core, chip], asend.at[i], arecv.at[col], (row, who)))
    own[core, chip] = hid[col]

    others = near if far is None else near + [far]

    def tok_at(q, of_chip):
        return toks[q // TILES].at[of_chip, q % TILES]

    def t_start(q):
        for i, other in enumerate(others):
            go(remote(
                tok_at(q, chip), tok_at(q, chip), tsend.at[q, i], trecv.at[q, chip], (row, other * CORES + core)
            ))

    def t_wait(q):
        for other in others:
            remote(
                tok_at(q, chip), tok_at(q, other), tsend.at[q, 0], trecv.at[q, other], (row, partner)
            ).wait_recv()

    w_near(0)
    for q in range(2, TILES):
        nearer(q)
    w_near(1)
    w_near(2)
    query_copy = remote(queries.at[0], queries.at[1], qsend, qrecv, (row, partner))

    def weights(q):
        return wbuf[q].reshape(chans, chans)

    def ask():
        for i in range(1, n_col):
            who = lax.rem(col + i, n_col)
            remote(
                hid.at[0], own.at[lax.rem(who, CORES), who // CORES], asend.at[i], arecv.at[who], (row, partner)
            ).wait_recv()
        local[2].wait()
        for q in range(3):
            w_settle(q)

        mine = jnp.concatenate(
            [jnp.concatenate([own[c, k] for k in range(n_chip)], axis=1) for c in range(CORES)], axis=0
        )

        query = lax.dot_general(mine, weights(0), NT, preferred_element_type=jnp.float32).astype(jnp.bfloat16)
        query = jnp.dot(query, weights(1), preferred_element_type=jnp.float32)
        queries[0] = (query * chans ** (-0.5)).astype(jnp.bfloat16)
        query_copy.start()

    for q in range(slots):
        if q + TILES < slots:
            nearer(q + TILES)
        farther(q)
        tok_at(q, chip)[...] = at(sels, q)[...] + at(up_ins, q)[...] + at(dn_ins, q)[...]
        t_start(q)
        if q == slots - 5:
            for k in range(3):
                w_far(k)
        if q == slots - 2:
            ask()
    query_copy.wait_recv()

    def keys_of(q):
        found = toks[q // TILES]
        size = TILE_DEV * found.shape[3]
        return jnp.concatenate([found[k, q % TILES].reshape(size, group) for k in range(n_chip)], axis=1)

    def attend(query, keys, state):
        score = lax.dot_general(query, keys, NT, preferred_element_type=jnp.float32)
        fresh = jnp.max(score, axis=1, keepdims=True)
        if state is not None:
            fresh = jnp.maximum(fresh, state[0])
        weight = jnp.exp(score - fresh)
        total = jnp.sum(weight, axis=1, keepdims=True)
        accum = jnp.dot(weight.astype(jnp.bfloat16), keys, preferred_element_type=jnp.float32)
        if state is not None:
            factor = jnp.exp(state[0] - fresh)
            total = total + state[1] * factor
            accum = accum + state[2] * factor
        return fresh, total, accum

    steps = [range(t, t + TILES) for t in range(0, slots - TILES, TILES)]
    steps += [range(t, t + TILES // 2) for t in (slots - TILES, slots - TILES // 2)]
    states = [None, None]
    for t, step in enumerate(steps):
        for q in step:
            t_wait(q)
        keys = jnp.concatenate([keys_of(q) for q in step], axis=0)
        states[1] = attend(queries[1], keys, states[1])
        if t == len(steps) - 1:
            peak, total, accum = states[1]
            share_out[:, :chans] = accum
            share_out[:, chans:chans + 128] = jnp.broadcast_to(peak, (rows * cols, 128))
            share_out[:, chans + 128:] = jnp.broadcast_to(total, (rows * cols, 128))
            share_copy = remote(share_out, share_in, ssend, srecv, (row, partner))
            share_copy.start()
        states[0] = attend(queries[0], keys, states[0])
    peak, total, accum = states[0]
    share_copy.wait_recv()
    its_peak, its_total = share_in[:, chans:chans + 1], share_in[:, chans + 128:chans + 129]
    fresh = jnp.maximum(peak, its_peak)
    mine, its = jnp.exp(peak - fresh), jnp.exp(its_peak - fresh)
    total = total * mine + its_total * its
    accum = accum * mine + share_in[:, :chans] * its
    context = (accum / total).astype(jnp.bfloat16)
    attended = lax.dot_general(context, weights(2), NT, preferred_element_type=jnp.float32)
    local[1].wait()
    out_ref[...] = (lat[...].astype(jnp.float32) + attended.reshape(rows, cols, chans)).astype(out_ref.dtype)

    for to_core in range(CORES):

        @pl.when(core == 1 - to_core)
        def _():
            for p in range(parts):
                to_partner(p, to_core).wait_send()

    taps_copy.wait_send()
    query_copy.wait_send()
    share_copy.wait_send()

    def edge_sent(to_core):
        for i in range(len(near)):
            edge_out(to_core, i).wait_send()

        @pl.when(core != to_core)
        def _():
            edge_out(to_core, len(near)).wait_send()

    on_edges(edge_sent)
    if far is not None:
        for p in range(parts):
            for k in range(2):
                relayed(p, k, early[k])
        for k in range(2):
            on_my_edge(lambda to_core: edge_relay(k, early[k], near[1 - k])(to_core).wait_send())

    @pl.when(has_down)
    def _():
        z_copy(0).wait_send()
        for q in range(slots):
            up_copy(q).wait_send()

    @pl.when(has_up)
    def _():
        z_copy(1).wait_send()
        for q in range(slots):
            dn_copy(q).wait_send()

    for copy in sends:
        copy.wait_send()


def vmem():
    return pl.BlockSpec(memory_space=pltpu.VMEM)


def anywhere():
    return pl.BlockSpec(memory_space=pl.ANY)


def body(n_row, n_col, latents, w_conv, conv_bias, w_qkv, owners):
    rows, cols, chans = latents.shape
    width = w_conv.shape[3]
    n_chip = n_col // CORES
    group, half = width * CORES, rows // CORES
    first = half // 4 * 2 + 2
    spans = (first, half - first)
    count, slots, parts = half * cols, len(spans) * TILES, len(spans)
    dma = pltpu.SemaphoreType.DMA
    bf16 = jnp.bfloat16
    line = tuple(pltpu.VMEM((TILES, TILE_DEV, span * cols, group), bf16) for span in spans)
    tokens = tuple(pltpu.VMEM((n_chip, TILES, TILE_DEV, span * cols, group), bf16) for span in spans)
    return pl.pallas_call(
        functools.partial(block_kernel, n_row, n_col, spans),
        out_shape=pltpu.VMEM((rows, cols, chans), bf16),
        in_specs=[anywhere()] * 5,
        out_specs=vmem(),
        scratch_shapes=[
            pltpu.SMEM((TILES,), jnp.int32),
            pltpu.VMEM((1, chans), jnp.float32),
            pltpu.VMEM((n_col, half + 2, cols, chans), bf16),
            pltpu.VMEM((rows, cols, chans), bf16),
            pltpu.VMEM((2, cols, chans), bf16),
            pltpu.VMEM((3, 3, CORES, width, chans), bf16),
            pltpu.VMEM((n_col, half, cols, 3 * group), jnp.float32),
            pltpu.VMEM((n_col, count, group), bf16),
            line, line, line, line, line, tokens,
            pltpu.VMEM((CORES, n_chip, count, group), bf16),
            pltpu.VMEM((3, n_col, width, chans), bf16),
            pltpu.VMEM((CORES, rows * cols, chans), bf16),
            pltpu.VMEM((rows * cols, chans + 256), jnp.float32),
            pltpu.VMEM((rows * cols, chans + 256), jnp.float32),
            dma((6 + parts,)), dma((parts, max(n_chip - 1, 3), CORES)), dma((parts, n_col)),
            dma((2,)), dma((2,)), dma((2, n_chip)), dma((n_col,)), dma((3 + parts,)), dma,
            dma((slots,)), dma((slots,)), dma((slots,)), dma((slots,)),
            dma((slots, n_chip)), dma((slots, n_chip)), dma, dma, dma, dma,
            dma((n_col,)), dma((n_col,)),
            dma((3, n_chip)), dma((3, n_col)), dma((3, n_chip)),
        ],
        compiler_params=pltpu.CompilerParams(
            collective_id=0, has_side_effects=True, vmem_limit_bytes=VMEM_LIMIT
        ),
    )(
        owners, latents, jnp.transpose(w_conv, (0, 1, 3, 2)), conv_bias.reshape(1, chans),
        jnp.transpose(w_qkv, (0, 2, 1)),
    )


def solution(mesh):
    placed = (P("row", "col", None), P(None, None, None, "col"), P(), P(None, None, "col"), P())
    return jax.shard_map(
        functools.partial(body, mesh.shape["row"], mesh.shape["col"]),
        mesh=mesh, in_specs=placed, out_specs=P("row", "col", None), check_vma=False,
    )
```

```python
import functools

import jax
import jax.numpy as jnp
from jax import lax
from jax.experimental import pallas as pl
from jax.experimental.pallas import tpu as pltpu
from jax.sharding import PartitionSpec as P

TILES = 4
TILE_DEV = 2
CORES = 2
MESH = pl.DeviceIdType.MESH
VMEM_LIMIT = 56 * 1024 * 1024
NT = (((1,), (1,)), ((), ()))


def remote(src, dst, send, recv, target):
    return pltpu.make_async_remote_copy(
        src_ref=src, dst_ref=dst, send_sem=send, recv_sem=recv, device_id=target, device_id_type=MESH
    )


def chips_around(chip, n_chip):
    if n_chip == 4:
        beside = chip + 1 - 2 * lax.rem(chip, 2)
        across = lax.rem(chip + 2, n_chip)
        return [beside, across], lax.rem(beside + 2, n_chip)
    return [lax.rem(chip + i, n_chip) for i in range(1, n_chip)], None


def spread(row, col, n_col, src, place, send, recv, fsend, sends):
    chip, core = col // CORES, lax.rem(col, CORES)
    n_chip = n_col // CORES
    partner = chip * CORES + 1 - core
    near, far = chips_around(chip, n_chip)

    def go(source, target, send_sem, recv_sem, device):
        copy = remote(source, target, send_sem, recv_sem, (row, device))
        copy.start()
        sends.append(copy)

    def start(q):
        for i, other in enumerate(near if q % 2 == 0 else near[::-1]):
            go(src(q), place(q, col), send.at[q, i], recv.at[q, col], other * CORES + core)
        go(src(q), place(q, col), fsend.at[q, chip], recv.at[q, col], partner)

    def wait(q, who):
        remote(src(q), place(q, who), fsend.at[q, chip], recv.at[q, who], (row, partner)).wait_recv()

    def forward(q, origin):
        who = origin * CORES + core
        go(place(q, who), place(q, who), fsend.at[q, origin], recv.at[q, who], partner)

    def pass_near(q):
        order = near if q % 2 == 0 else near[::-1]
        for k, origin in enumerate(order):
            who = origin * CORES + core
            wait(q, who)
            if far is not None and k == 0:
                go(place(q, who), place(q, who), send.at[q, 2], recv.at[q, who], order[1] * CORES + core)
            forward(q, origin)

    def pass_far(q):
        if far is not None:
            wait(q, far * CORES + core)
            forward(q, far)

    def settle(q):
        for i in range(n_chip):
            wait(q, lax.rem(chip + i, n_chip) * CORES + 1 - core)

    return start, pass_near, pass_far, settle


def block_kernel(
    n_row, n_col, spans, owners_hbm, lat_ref, taps_ref, bias_hbm, w_ref, out_ref,
    owners_ref, bias_ref, img, lat, edges, taps, wide, hid,
    sels, up_ins, up_outs, dn_ins, dn_outs, toks, own, wbuf, queries, share_out, share_in, level_out, level_in,
    lsem, isend, irecv, zsend, zrecv, hsend, hrecv, csend, crecv,
    up_send, up_recv, dn_send, dn_recv, tsend, trecv, qsend, qrecv, ssend, srecv,
    asend, arecv, wsend, wrecv, wfsend,
):
    row, col = lax.axis_index("row"), lax.axis_index("col")
    chip, core = col // CORES, lax.rem(col, CORES)
    n_chip = n_col // CORES
    partner = chip * CORES + 1 - core
    near, far = chips_around(chip, n_chip)
    rows, cols, chans = lat_ref.shape
    half = rows // CORES
    group = hid.shape[2]
    count = half * cols
    parts = len(spans)
    starts = [sum(spans[:p]) for p in range(parts)]
    slots = parts * TILES
    has_up, has_down = row > 0, row < n_row - 1
    top = core == 0

    barrier = pltpu.get_barrier_semaphore()

    def hello(target):
        pl.semaphore_signal(barrier, inc=1, device_id=target, device_id_type=MESH)

    @pl.when(has_up)
    def _():
        hello((row - 1, col))

    @pl.when(has_down)
    def _():
        hello((row + 1, col))

    for other in near:
        for c in range(CORES):
            hello((row, other * CORES + c))
    hello((row, partner))

    inner = tuple(start + 2 for start in starts[1:])
    own_rows = ((1, *inner, half + 2), (0, *inner, half + 1))

    def piece(p, to_core, who=None):
        lo, hi = own_rows[to_core][p], own_rows[to_core][p + 1]
        if who is None:
            return lat_ref.at[pl.ds(lo - 1 + to_core * half, hi - lo)]
        return img.at[who, pl.ds(lo, hi - lo)]

    local = [
        pltpu.make_async_copy(taps_ref, taps.at[:, :, core], lsem.at[0]),
        pltpu.make_async_copy(lat_ref, lat, lsem.at[1]),
        pltpu.make_async_copy(w_ref, wbuf.at[:, col], lsem.at[2]),
        pltpu.make_async_copy(bias_hbm, bias_ref, lsem.at[3]),
        pltpu.make_async_copy(owners_hbm, owners_ref, lsem.at[4]),
    ]

    def edge_row(to_core):
        return 0 if to_core == 0 else half + 1

    @pl.when(jnp.logical_and(top, jnp.logical_not(has_up)))
    def _():
        for who in range(n_col):
            img[who, edge_row(0)] = jnp.zeros((cols, chans), img.dtype)

    @pl.when(jnp.logical_and(jnp.logical_not(top), jnp.logical_not(has_down)))
    def _():
        for who in range(n_col):
            img[who, edge_row(1)] = jnp.zeros((cols, chans), img.dtype)

    pl.semaphore_wait(barrier, CORES * len(near) + 1 + has_up.astype(jnp.int32) + has_down.astype(jnp.int32))

    sends = []

    def go(copy):
        copy.start()
        sends.append(copy)

    def z_copy(to_core):
        if to_core == 0:
            return remote(lat_ref.at[rows - 1], edges.at[0], zsend.at[0], zrecv.at[0], (row + 1, col))
        return remote(lat_ref.at[0], edges.at[1], zsend.at[1], zrecv.at[1], (row - 1, col))

    @pl.when(has_down)
    def _():
        z_copy(0).start()

    @pl.when(has_up)
    def _():
        z_copy(1).start()

    def image(p, i, other):
        for to_core in range(CORES):
            go(remote(
                piece(p, to_core), piece(p, to_core, col), isend.at[p, i, to_core], irecv.at[p, col],
                (row, other * CORES + to_core),
            ))

    if far is None:
        order = near
    else:
        order = [jnp.where(top, near[0], near[1]), jnp.where(top, near[1], near[0])]
    for i, other in enumerate(order):
        image(0, i, other)

    taps_copy = remote(taps_ref, taps.at[:, :, core], csend.at[0], crecv, (row, partner))
    taps_copy.start()
    local[0].start()

    def to_partner(p, to_core):
        return remote(
            piece(p, to_core), piece(p, to_core, col), csend.at[3 + p], irecv.at[p, col], (row, chip * CORES + to_core)
        )

    def to_self(p, to_core):
        return pltpu.make_async_copy(piece(p, to_core), piece(p, to_core, col), lsem.at[6 + p])

    for to_core in range(CORES):

        @pl.when(core == to_core)
        def _():
            for p in range(parts):
                to_self(p, to_core).start()

        @pl.when(core == 1 - to_core)
        def _():
            for p in range(parts):
                to_partner(p, to_core).start()

    for copy in local[1:]:
        copy.start()

    def edge_place(to_core, who):
        return img.at[who, edge_row(to_core)]

    def edge_out(to_core, i):
        if i < len(near):
            target = near[i] * CORES + to_core
        else:
            target = partner
        return remote(
            edges.at[to_core], edge_place(to_core, col), hsend.at[to_core, i], hrecv.at[col], (row, target)
        )

    def edge_self(to_core):
        return pltpu.make_async_copy(edges.at[to_core], edge_place(to_core, col), lsem.at[5])

    def on_edges(act):
        for to_core in range(CORES):

            @pl.when(has_up if to_core == 0 else has_down)
            def _():
                act(to_core)

    def edge_spread(to_core):
        z_copy(to_core).wait_recv()
        for i in range(len(near)):
            edge_out(to_core, i).start()

        @pl.when(core == to_core)
        def _():
            edge_self(to_core).start()

        @pl.when(core != to_core)
        def _():
            edge_out(to_core, len(near)).start()

    on_edges(edge_spread)

    def on_my_edge(act):
        for to_core in range(CORES):

            @pl.when(jnp.logical_and(core == to_core, has_up if to_core == 0 else has_down))
            def _():
                act(to_core)

    def edge_in(who):
        on_my_edge(lambda to_core: remote(
            edges.at[to_core], edge_place(to_core, who), csend.at[0], hrecv.at[who], (row, partner)
        ).wait_recv())

    def strip_in(p, who):
        for to_core in range(CORES):

            @pl.when(core == to_core)
            def _():
                remote(
                    piece(p, to_core, who), piece(p, to_core, who), csend.at[0], irecv.at[p, who], (row, partner)
                ).wait_recv()

    def relay(p, k, who, target):
        for to_core in range(CORES):

            @pl.when(core == to_core)
            def _():
                remote(
                    piece(p, to_core, who), piece(p, to_core, who), isend.at[p, 2, k], irecv.at[p, who],
                    (row, target * CORES + to_core),
                ).start()

    def relayed(p, k, who):
        for to_core in range(CORES):

            @pl.when(core == to_core)
            def _():
                remote(
                    piece(p, to_core, who), piece(p, to_core, who), isend.at[p, 2, k], irecv.at[p, who],
                    (row, partner),
                ).wait_send()

    def edge_relay(k, who, target):
        return lambda to_core: remote(
            edge_place(to_core, who), edge_place(to_core, who), csend.at[1 + k], hrecv.at[who],
            (row, target * CORES + to_core),
        )

    def convolve(p, group_of):
        size = spans[p] * cols
        total = None
        for tap in range(3):
            window = jnp.concatenate(
                [img[who, pl.ds(starts[p] + tap, spans[p])].reshape(size, chans) for who in group_of], axis=0
            )
            kernel = taps[tap].reshape(3 * group, chans)
            part = lax.dot_general(window, kernel, NT, preferred_element_type=jnp.float32)
            total = part if total is None else total + part
        for i, who in enumerate(group_of):
            wide[who, pl.ds(starts[p], spans[p])] = total[i * size:(i + 1) * size].reshape(
                spans[p], cols, 3 * group
            )

    def finish(p):
        bias = None
        for k in range(n_chip):
            mine = jnp.where(chip == k, bias_ref[:, k * group:(k + 1) * group], 0.0)
            bias = mine if bias is None else bias + mine
        bias = bias.reshape(1, 1, group)
        shape = (spans[p], cols, group)
        at = lax.broadcasted_iota(jnp.int32, shape, 1)

        def part_of(who, tap):
            return wide[who, pl.ds(starts[p], spans[p]), :, pl.ds(tap * group, group)]

        previous = jnp.zeros(shape, jnp.float32)
        after = pltpu.roll(part_of(0, 2), cols - 1, 1)
        for who in range(n_col):
            left = pltpu.roll(part_of(who, 0), 1, 1)
            right = after
            if who + 1 < n_col:
                after = pltpu.roll(part_of(who + 1, 2), cols - 1, 1)
            else:
                after = jnp.zeros(shape, jnp.float32)
            conv = part_of(who, 1) + jnp.where(at == 0, previous, left) + jnp.where(at == cols - 1, after, right)
            previous = left
            conv = (conv + bias).reshape(spans[p] * cols, group)
            hid[who, pl.ds(starts[p] * cols, spans[p] * cols)] = (conv * jax.nn.sigmoid(conv)).astype(hid.dtype)

    def at(pair, q):
        return pair[q // TILES].at[q % TILES]

    def up_copy(q):
        return remote(at(up_outs, q), at(up_ins, q), up_send.at[q], up_recv.at[q], (row + 1, col))

    def dn_copy(q):
        return remote(at(dn_outs, q), at(dn_ins, q), dn_send.at[q], dn_recv.at[q], (row - 1, col))

    def select(p):
        for tile in range(TILES):
            q = p * TILES + tile
            flat = TILE_DEV * owners_ref[tile]
            here = flat // n_col == row
            for member in range(TILE_DEV):
                block = hid[lax.rem(flat, n_col) + member, pl.ds(starts[p] * cols, spans[p] * cols)]
                block = jnp.where(here, block, jnp.zeros_like(block))
                for kept in (sels, up_outs, dn_outs):
                    at(kept, q)[member] = block

            @pl.when(jnp.logical_not(has_up))
            def _():
                up_copy(q).start()
                at(up_ins, q)[...] = jnp.zeros(up_ins[p].shape[1:], hid.dtype)

            @pl.when(jnp.logical_not(has_down))
            def _():
                dn_copy(q).start()
                at(dn_ins, q)[...] = jnp.zeros(dn_ins[p].shape[1:], hid.dtype)

    w_start, w_near, w_far, w_settle = spread(
        row, col, n_col, lambda q: w_ref.at[q], lambda q, who: wbuf.at[q, who],
        wsend, wrecv, wfsend, sends,
    )

    def mine_in(p):
        for to_core in range(CORES):

            @pl.when(core == to_core)
            def _():
                to_self(p, to_core).wait()

        strip_in(p, partner)

    def edges_in(group_of):
        for who in group_of:
            if who is col:
                on_my_edge(lambda to_core: edge_self(to_core).wait())
            else:
                edge_in(who)

    lower = row < n_row // 2

    def upward(q, cond):
        @pl.when(jnp.logical_and(cond, has_up))
        def _():
            up_copy(q).wait_recv()

            @pl.when(has_down)
            def _():
                at(up_outs, q)[...] = at(sels, q)[...] + at(up_ins, q)[...]
                up_copy(q).start()

    def downward(q, cond):
        @pl.when(jnp.logical_and(cond, has_down))
        def _():
            dn_copy(q).wait_recv()

            @pl.when(has_up)
            def _():
                at(dn_outs, q)[...] = at(sels, q)[...] + at(dn_ins, q)[...]
                dn_copy(q).start()

    def nearer(q):
        upward(q, lower)
        downward(q, jnp.logical_not(lower))

    def farther(q):
        downward(q, lower)
        upward(q, jnp.logical_not(lower))

    pair = (col, partner)
    if far is None:
        local[0].wait()
        taps_copy.wait_recv()
        edges_in(pair)
        for p in range(1, parts):
            for i, other in enumerate(order):
                image(p, i, other)
        for q in range(3):
            w_start(q)
        for p in range(parts):
            mine_in(p)
            convolve(p, pair)

            def other_chip(i, _):
                other = lax.rem(chip + i, n_chip)
                for who in (other * CORES, other * CORES + 1):
                    strip_in(p, who)
                    if p == 0:
                        edge_in(who)
                convolve(p, (other * CORES, other * CORES + 1))
                return 0

            lax.fori_loop(1, n_chip, other_chip, 0)
            if p == 0:
                for copy in local[3:]:
                    copy.wait()
            finish(p)
            select(p)
            if p == parts - 2:
                for q in range(TILES):
                    nearer(q)
    else:
        early = (near[0] * CORES, near[1] * CORES + 1)
        late = (near[0] * CORES + 1, near[1] * CORES)
        last = (far * CORES, far * CORES + 1)

        def relay_early(p):
            for k in range(2):
                strip_in(p, early[k])
                relay(p, k, early[k], near[1 - k])
                if p == 0:
                    edge_in(early[k])
                    on_my_edge(lambda to_core: edge_relay(k, early[k], near[1 - k])(to_core).start())

        for p in range(parts):
            if p + 1 < parts:
                image(p + 1, 0, order[0])
            if p < parts - 1:
                relay_early(p)
            if p + 1 < parts:
                image(p + 1, 1, order[1])
        local[0].wait()
        taps_copy.wait_recv()
        edges_in(pair)
        for p in range(parts):
            mine_in(p)
            convolve(p, pair + early)
            if p == parts - 2:
                relay_early(parts - 1)
                for q in range(3):
                    w_start(q)
            for group_of in (late, last):
                for who in group_of:
                    strip_in(p, who)
                    if p == 0:
                        edge_in(who)
                convolve(p, group_of)
            if p == 0:
                for copy in local[3:]:
                    copy.wait()
            if p == parts - 1:
                nearer(0)
                nearer(1)
            finish(p)
            select(p)

    for i in range(1, n_col):
        who = lax.rem(col + i, n_col)
        go(remote(hid.at[who], own.at[core, chip], asend.at[i], arecv.at[col], (row, who)))
    own[core, chip] = hid[col]

    others = near if far is None else [far] + near

    def tok_at(q, of_chip):
        return toks[q // TILES].at[of_chip, q % TILES]

    def t_start(q):
        for i, other in enumerate(others):
            go(remote(
                tok_at(q, chip), tok_at(q, chip), tsend.at[q, i], trecv.at[q, chip], (row, other * CORES + core)
            ))

    def t_wait(q):
        for other in others:
            remote(
                tok_at(q, chip), tok_at(q, other), tsend.at[q, 0], trecv.at[q, other], (row, partner)
            ).wait_recv()

    for q in range(2, TILES):
        nearer(q)
    w_near(0)
    w_near(1)
    w_near(2)
    query_copy = remote(queries.at[0], queries.at[1], qsend, qrecv, (row, partner))

    def weights(q):
        return wbuf[q].reshape(chans, chans)

    def ask():
        for i in range(1, n_col):
            who = lax.rem(col + i, n_col)
            remote(
                hid.at[0], own.at[lax.rem(who, CORES), who // CORES], asend.at[i], arecv.at[who], (row, partner)
            ).wait_recv()
        local[2].wait()
        for q in range(3):
            w_settle(q)

        mine = jnp.concatenate(
            [jnp.concatenate([own[c, k] for k in range(n_chip)], axis=1) for c in range(CORES)], axis=0
        )

        query = lax.dot_general(mine, weights(0), NT, preferred_element_type=jnp.float32).astype(jnp.bfloat16)
        query = jnp.dot(query, weights(1), preferred_element_type=jnp.float32)
        queries[0] = (query * chans ** (-0.5)).astype(jnp.bfloat16)
        query_copy.start()

    for q in range(slots):
        if q + TILES < slots:
            nearer(q + TILES)
        farther(q)
        tok_at(q, chip)[...] = at(sels, q)[...] + at(up_ins, q)[...] + at(dn_ins, q)[...]
        t_start(q)
        if q == slots - 5:
            for k in range(3):
                w_far(k)
        if q == slots - 2:
            ask()
    query_copy.wait_recv()

    def keys_of(q):
        found = toks[q // TILES]
        size = TILE_DEV * found.shape[3]
        return jnp.concatenate([found[k, q % TILES].reshape(size, group) for k in range(n_chip)], axis=1)

    def attend(query, keys, state):
        score = lax.dot_general(query, keys, NT, preferred_element_type=jnp.float32)
        fresh = jnp.max(score, axis=1, keepdims=True)
        if state is not None:
            fresh = jnp.maximum(fresh, state[0])
        weight = jnp.exp(score - fresh)
        total = jnp.sum(weight, axis=1, keepdims=True)
        accum = jnp.dot(weight.astype(jnp.bfloat16), keys, preferred_element_type=jnp.float32)
        if state is not None:
            factor = jnp.exp(state[0] - fresh)
            total = total + state[1] * factor
            accum = accum + state[2] * factor
        return fresh, total, accum

    steps = [range(t, t + TILES) for t in range(0, slots - TILES, TILES)]
    steps += [range(t, t + TILES // 2) for t in (slots - TILES, slots - TILES // 2)]
    states = [None, None]
    for t, step in enumerate(steps):
        for q in step:
            t_wait(q)
        keys = jnp.concatenate([keys_of(q) for q in step], axis=0)
        states[1] = attend(queries[1], keys, states[1])
        if t == len(steps) - 1:
            peak, total, accum = states[1]
            share_out[...] = (accum / total).astype(share_out.dtype)
            level_out[...] = jnp.broadcast_to(peak + jnp.log(total), level_out.shape)
            share_copies = [
                remote(share_out, share_in, ssend.at[0], srecv.at[0], (row, partner)),
                remote(level_out, level_in, ssend.at[1], srecv.at[1], (row, partner)),
            ]
            for copy in share_copies:
                copy.start()
        states[0] = attend(queries[0], keys, states[0])
    peak, total, accum = states[0]
    level, context = peak + jnp.log(total), accum / total
    for copy in share_copies:
        copy.wait_recv()
    keep = 1.0 / (1.0 + jnp.exp(level_in[:, :1] - level))
    context = context * keep + share_in[...].astype(jnp.float32) * (1.0 - keep)
    context = context.astype(jnp.bfloat16)
    attended = lax.dot_general(context, weights(2), NT, preferred_element_type=jnp.float32)
    local[1].wait()
    out_ref[...] = (lat[...].astype(jnp.float32) + attended.reshape(rows, cols, chans)).astype(out_ref.dtype)

    for to_core in range(CORES):

        @pl.when(core == 1 - to_core)
        def _():
            for p in range(parts):
                to_partner(p, to_core).wait_send()

    taps_copy.wait_send()
    query_copy.wait_send()
    for copy in share_copies:
        copy.wait_send()

    def edge_sent(to_core):
        for i in range(len(near)):
            edge_out(to_core, i).wait_send()

        @pl.when(core != to_core)
        def _():
            edge_out(to_core, len(near)).wait_send()

    on_edges(edge_sent)
    if far is not None:
        for p in range(parts):
            for k in range(2):
                relayed(p, k, early[k])
        for k in range(2):
            on_my_edge(lambda to_core: edge_relay(k, early[k], near[1 - k])(to_core).wait_send())

    @pl.when(has_down)
    def _():
        z_copy(0).wait_send()
        for q in range(slots):
            up_copy(q).wait_send()

    @pl.when(has_up)
    def _():
        z_copy(1).wait_send()
        for q in range(slots):
            dn_copy(q).wait_send()

    for copy in sends:
        copy.wait_send()


def vmem():
    return pl.BlockSpec(memory_space=pltpu.VMEM)


def anywhere():
    return pl.BlockSpec(memory_space=pl.ANY)


def body(n_row, n_col, latents, w_conv, conv_bias, w_qkv, owners):
    rows, cols, chans = latents.shape
    width = w_conv.shape[3]
    n_chip = n_col // CORES
    group, half = width * CORES, rows // CORES
    first = half // 4 * 2 + 2
    spans = (first, half - first)
    count, slots, parts = half * cols, len(spans) * TILES, len(spans)
    dma = pltpu.SemaphoreType.DMA
    bf16 = jnp.bfloat16
    line = tuple(pltpu.VMEM((TILES, TILE_DEV, span * cols, group), bf16) for span in spans)
    tokens = tuple(pltpu.VMEM((n_chip, TILES, TILE_DEV, span * cols, group), bf16) for span in spans)
    return pl.pallas_call(
        functools.partial(block_kernel, n_row, n_col, spans),
        out_shape=pltpu.VMEM((rows, cols, chans), bf16),
        in_specs=[anywhere()] * 5,
        out_specs=vmem(),
        scratch_shapes=[
            pltpu.SMEM((TILES,), jnp.int32),
            pltpu.VMEM((1, chans), jnp.float32),
            pltpu.VMEM((n_col, half + 2, cols, chans), bf16),
            pltpu.VMEM((rows, cols, chans), bf16),
            pltpu.VMEM((2, cols, chans), bf16),
            pltpu.VMEM((3, 3, CORES, width, chans), bf16),
            pltpu.VMEM((n_col, half, cols, 3 * group), jnp.float32),
            pltpu.VMEM((n_col, count, group), bf16),
            line, line, line, line, line, tokens,
            pltpu.VMEM((CORES, n_chip, count, group), bf16),
            pltpu.VMEM((3, n_col, width, chans), bf16),
            pltpu.VMEM((CORES, rows * cols, chans), bf16),
            pltpu.VMEM((rows * cols, chans), bf16),
            pltpu.VMEM((rows * cols, chans), bf16),
            pltpu.VMEM((rows * cols, 128), jnp.float32),
            pltpu.VMEM((rows * cols, 128), jnp.float32),
            dma((6 + parts,)), dma((parts, max(n_chip - 1, 3), CORES)), dma((parts, n_col)),
            dma((2,)), dma((2,)), dma((2, n_chip)), dma((n_col,)), dma((3 + parts,)), dma,
            dma((slots,)), dma((slots,)), dma((slots,)), dma((slots,)),
            dma((slots, n_chip)), dma((slots, n_chip)), dma, dma, dma((2,)), dma((2,)),
            dma((n_col,)), dma((n_col,)),
            dma((3, n_chip)), dma((3, n_col)), dma((3, n_chip)),
        ],
        compiler_params=pltpu.CompilerParams(
            collective_id=0, has_side_effects=True, vmem_limit_bytes=VMEM_LIMIT
        ),
    )(
        owners, latents, jnp.transpose(w_conv, (0, 1, 3, 2)), conv_bias.reshape(1, chans),
        jnp.transpose(w_qkv, (0, 2, 1)),
    )


def solution(mesh):
    placed = (P("row", "col", None), P(None, None, None, "col"), P(), P(None, None, "col"), P())
    return jax.shard_map(
        functools.partial(body, mesh.shape["row"], mesh.shape["col"]),
        mesh=mesh, in_specs=placed, out_specs=P("row", "col", None), check_vma=False,
    )
```

```python
import functools

import jax
import jax.numpy as jnp
from jax import lax
from jax.experimental import pallas as pl
from jax.experimental.pallas import tpu as pltpu
from jax.sharding import PartitionSpec as P

TILES = 4
TILE_DEV = 2
CORES = 2
MESH = pl.DeviceIdType.MESH
VMEM_LIMIT = 56 * 1024 * 1024
NT = (((1,), (1,)), ((), ()))


def remote(src, dst, send, recv, target):
    return pltpu.make_async_remote_copy(
        src_ref=src, dst_ref=dst, send_sem=send, recv_sem=recv, device_id=target, device_id_type=MESH
    )


def chips_around(chip, n_chip):
    if n_chip == 4:
        beside = chip + 1 - 2 * lax.rem(chip, 2)
        across = lax.rem(chip + 2, n_chip)
        return [beside, across], lax.rem(beside + 2, n_chip)
    return [lax.rem(chip + i, n_chip) for i in range(1, n_chip)], None


def spread(row, col, n_col, src, place, send, recv, fsend, sends):
    chip, core = col // CORES, lax.rem(col, CORES)
    n_chip = n_col // CORES
    partner = chip * CORES + 1 - core
    near, far = chips_around(chip, n_chip)

    def go(source, target, send_sem, recv_sem, device):
        copy = remote(source, target, send_sem, recv_sem, (row, device))
        copy.start()
        sends.append(copy)

    def start(q):
        for i, other in enumerate(near if q % 2 == 0 else near[::-1]):
            go(src(q), place(q, col), send.at[q, i], recv.at[q, col], other * CORES + core)
        go(src(q), place(q, col), fsend.at[q, chip], recv.at[q, col], partner)

    def wait(q, who):
        remote(src(q), place(q, who), fsend.at[q, chip], recv.at[q, who], (row, partner)).wait_recv()

    def forward(q, origin):
        who = origin * CORES + core
        go(place(q, who), place(q, who), fsend.at[q, origin], recv.at[q, who], partner)

    def pass_near(q):
        order = near if q % 2 == 0 else near[::-1]
        for k, origin in enumerate(order):
            who = origin * CORES + core
            wait(q, who)
            if far is not None and k == 0:
                go(place(q, who), place(q, who), send.at[q, 2], recv.at[q, who], order[1] * CORES + core)
            forward(q, origin)

    def pass_far(q):
        if far is not None:
            wait(q, far * CORES + core)
            forward(q, far)

    def settle(q):
        for i in range(n_chip):
            wait(q, lax.rem(chip + i, n_chip) * CORES + 1 - core)

    return start, pass_near, pass_far, settle


def block_kernel(
    n_row, n_col, spans, owners_hbm, lat_ref, taps_ref, bias_hbm, w_ref, out_ref,
    owners_ref, bias_ref, img, lat, edges, taps, wide, hid,
    sels, up_ins, up_outs, dn_ins, dn_outs, toks, own, wbuf, queries, share_out, share_in, level_out, level_in,
    lsem, isend, irecv, zsend, zrecv, hsend, hrecv, csend, crecv,
    up_send, up_recv, dn_send, dn_recv, tsend, trecv, qsend, qrecv, ssend, srecv,
    asend, arecv, wsend, wrecv, wfsend,
):
    row, col = lax.axis_index("row"), lax.axis_index("col")
    chip, core = col // CORES, lax.rem(col, CORES)
    n_chip = n_col // CORES
    partner = chip * CORES + 1 - core
    near, far = chips_around(chip, n_chip)
    rows, cols, chans = lat_ref.shape
    half = rows // CORES
    group = hid.shape[2]
    count = half * cols
    parts = len(spans)
    starts = [sum(spans[:p]) for p in range(parts)]
    slots = parts * TILES
    has_up, has_down = row > 0, row < n_row - 1
    top = core == 0

    barrier = pltpu.get_barrier_semaphore()

    def hello(target):
        pl.semaphore_signal(barrier, inc=1, device_id=target, device_id_type=MESH)

    @pl.when(has_up)
    def _():
        hello((row - 1, col))

    @pl.when(has_down)
    def _():
        hello((row + 1, col))

    for other in near:
        for c in range(CORES):
            hello((row, other * CORES + c))
    hello((row, partner))

    inner = tuple(start + 2 for start in starts[1:])
    own_rows = ((1, *inner, half + 2), (0, *inner, half + 1))

    def piece(p, to_core, who=None):
        lo, hi = own_rows[to_core][p], own_rows[to_core][p + 1]
        if who is None:
            return lat_ref.at[pl.ds(lo - 1 + to_core * half, hi - lo)]
        return img.at[who, pl.ds(lo, hi - lo)]

    local = [
        pltpu.make_async_copy(taps_ref, taps.at[:, :, core], lsem.at[0]),
        pltpu.make_async_copy(lat_ref, lat, lsem.at[1]),
        pltpu.make_async_copy(w_ref, wbuf.at[:, col], lsem.at[2]),
        pltpu.make_async_copy(bias_hbm, bias_ref, lsem.at[3]),
        pltpu.make_async_copy(owners_hbm, owners_ref, lsem.at[4]),
    ]

    def edge_row(to_core):
        return 0 if to_core == 0 else half + 1

    @pl.when(jnp.logical_and(top, jnp.logical_not(has_up)))
    def _():
        for who in range(n_col):
            img[who, edge_row(0)] = jnp.zeros((cols, chans), img.dtype)

    @pl.when(jnp.logical_and(jnp.logical_not(top), jnp.logical_not(has_down)))
    def _():
        for who in range(n_col):
            img[who, edge_row(1)] = jnp.zeros((cols, chans), img.dtype)

    pl.semaphore_wait(barrier, CORES * len(near) + 1 + has_up.astype(jnp.int32) + has_down.astype(jnp.int32))

    sends = []

    def go(copy):
        copy.start()
        sends.append(copy)

    def z_copy(to_core):
        if to_core == 0:
            return remote(lat_ref.at[rows - 1], edges.at[0], zsend.at[0], zrecv.at[0], (row + 1, col))
        return remote(lat_ref.at[0], edges.at[1], zsend.at[1], zrecv.at[1], (row - 1, col))

    @pl.when(has_down)
    def _():
        z_copy(0).start()

    @pl.when(has_up)
    def _():
        z_copy(1).start()

    def image(p, i, other):
        for to_core in range(CORES):
            go(remote(
                piece(p, to_core), piece(p, to_core, col), isend.at[p, i, to_core], irecv.at[p, col],
                (row, other * CORES + to_core),
            ))

    if far is None:
        order = near
    else:
        order = [jnp.where(top, near[0], near[1]), jnp.where(top, near[1], near[0])]
    for i, other in enumerate(order):
        image(0, i, other)

    taps_copy = remote(taps_ref, taps.at[:, :, core], csend.at[0], crecv, (row, partner))
    taps_copy.start()
    local[0].start()

    def to_partner(p, to_core):
        return remote(
            piece(p, to_core), piece(p, to_core, col), csend.at[3 + p], irecv.at[p, col], (row, chip * CORES + to_core)
        )

    def to_self(p, to_core):
        return pltpu.make_async_copy(piece(p, to_core), piece(p, to_core, col), lsem.at[6 + p])

    for to_core in range(CORES):

        @pl.when(core == to_core)
        def _():
            for p in range(parts):
                to_self(p, to_core).start()

        @pl.when(core == 1 - to_core)
        def _():
            for p in range(parts):
                to_partner(p, to_core).start()

    for copy in local[1:]:
        copy.start()

    def edge_place(to_core, who):
        return img.at[who, edge_row(to_core)]

    def edge_out(to_core, i):
        if i < len(near):
            target = near[i] * CORES + to_core
        else:
            target = partner
        return remote(
            edges.at[to_core], edge_place(to_core, col), hsend.at[to_core, i], hrecv.at[col], (row, target)
        )

    def edge_self(to_core):
        return pltpu.make_async_copy(edges.at[to_core], edge_place(to_core, col), lsem.at[5])

    def on_edges(act):
        for to_core in range(CORES):

            @pl.when(has_up if to_core == 0 else has_down)
            def _():
                act(to_core)

    def edge_spread(to_core):
        z_copy(to_core).wait_recv()
        for i in range(len(near)):
            edge_out(to_core, i).start()

        @pl.when(core == to_core)
        def _():
            edge_self(to_core).start()

        @pl.when(core != to_core)
        def _():
            edge_out(to_core, len(near)).start()

    on_edges(edge_spread)

    def on_my_edge(act):
        for to_core in range(CORES):

            @pl.when(jnp.logical_and(core == to_core, has_up if to_core == 0 else has_down))
            def _():
                act(to_core)

    def edge_in(who):
        on_my_edge(lambda to_core: remote(
            edges.at[to_core], edge_place(to_core, who), csend.at[0], hrecv.at[who], (row, partner)
        ).wait_recv())

    def strip_in(p, who):
        for to_core in range(CORES):

            @pl.when(core == to_core)
            def _():
                remote(
                    piece(p, to_core, who), piece(p, to_core, who), csend.at[0], irecv.at[p, who], (row, partner)
                ).wait_recv()

    def relay(p, k, who, target):
        for to_core in range(CORES):

            @pl.when(core == to_core)
            def _():
                remote(
                    piece(p, to_core, who), piece(p, to_core, who), isend.at[p, 2, k], irecv.at[p, who],
                    (row, target * CORES + to_core),
                ).start()

    def relayed(p, k, who):
        for to_core in range(CORES):

            @pl.when(core == to_core)
            def _():
                remote(
                    piece(p, to_core, who), piece(p, to_core, who), isend.at[p, 2, k], irecv.at[p, who],
                    (row, partner),
                ).wait_send()

    def edge_relay(k, who, target):
        return lambda to_core: remote(
            edge_place(to_core, who), edge_place(to_core, who), csend.at[1 + k], hrecv.at[who],
            (row, target * CORES + to_core),
        )

    def convolve(p, group_of):
        size = spans[p] * cols
        total = None
        for tap in range(3):
            window = jnp.concatenate(
                [img[who, pl.ds(starts[p] + tap, spans[p])].reshape(size, chans) for who in group_of], axis=0
            )
            kernel = taps[tap].reshape(3 * group, chans)
            part = lax.dot_general(window, kernel, NT, preferred_element_type=jnp.float32)
            total = part if total is None else total + part
        for i, who in enumerate(group_of):
            wide[who, pl.ds(starts[p], spans[p])] = total[i * size:(i + 1) * size].reshape(
                spans[p], cols, 3 * group
            )

    def finish(p):
        bias = None
        for k in range(n_chip):
            mine = jnp.where(chip == k, bias_ref[:, k * group:(k + 1) * group], 0.0)
            bias = mine if bias is None else bias + mine
        bias = bias.reshape(1, 1, group)
        shape = (spans[p], cols, group)
        at = lax.broadcasted_iota(jnp.int32, shape, 1)

        def part_of(who, tap):
            return wide[who, pl.ds(starts[p], spans[p]), :, pl.ds(tap * group, group)]

        previous = jnp.zeros(shape, jnp.float32)
        after = pltpu.roll(part_of(0, 2), cols - 1, 1)
        for who in range(n_col):
            left = pltpu.roll(part_of(who, 0), 1, 1)
            right = after
            if who + 1 < n_col:
                after = pltpu.roll(part_of(who + 1, 2), cols - 1, 1)
            else:
                after = jnp.zeros(shape, jnp.float32)
            conv = part_of(who, 1) + jnp.where(at == 0, previous, left) + jnp.where(at == cols - 1, after, right)
            previous = left
            conv = (conv + bias).reshape(spans[p] * cols, group)
            hid[who, pl.ds(starts[p] * cols, spans[p] * cols)] = (conv * jax.nn.sigmoid(conv)).astype(hid.dtype)

    def at(pair, q):
        return pair[q // TILES].at[q % TILES]

    def up_copy(q):
        return remote(at(up_outs, q), at(up_ins, q), up_send.at[q], up_recv.at[q], (row + 1, col))

    def dn_copy(q):
        return remote(at(dn_outs, q), at(dn_ins, q), dn_send.at[q], dn_recv.at[q], (row - 1, col))

    def select(p):
        for tile in range(TILES):
            q = p * TILES + tile
            flat = TILE_DEV * owners_ref[tile]
            here = flat // n_col == row
            for member in range(TILE_DEV):
                block = hid[lax.rem(flat, n_col) + member, pl.ds(starts[p] * cols, spans[p] * cols)]
                block = jnp.where(here, block, jnp.zeros_like(block))
                at(sels, q)[member] = block

            @pl.when(jnp.logical_not(has_up))
            def _():
                at(up_outs, q)[...] = at(sels, q)[...]
                up_copy(q).start()
                at(up_ins, q)[...] = jnp.zeros(up_ins[p].shape[1:], hid.dtype)

            @pl.when(jnp.logical_not(has_down))
            def _():
                at(dn_outs, q)[...] = at(sels, q)[...]
                dn_copy(q).start()
                at(dn_ins, q)[...] = jnp.zeros(dn_ins[p].shape[1:], hid.dtype)

    w_start, w_near, w_far, w_settle = spread(
        row, col, n_col, lambda q: w_ref.at[q], lambda q, who: wbuf.at[q, who],
        wsend, wrecv, wfsend, sends,
    )

    def mine_in(p):
        for to_core in range(CORES):

            @pl.when(core == to_core)
            def _():
                to_self(p, to_core).wait()

        strip_in(p, partner)

    def edges_in(group_of):
        for who in group_of:
            if who is col:
                on_my_edge(lambda to_core: edge_self(to_core).wait())
            else:
                edge_in(who)

    lower = row < n_row // 2

    def upward(q, cond):
        @pl.when(jnp.logical_and(cond, has_up))
        def _():
            up_copy(q).wait_recv()

            @pl.when(has_down)
            def _():
                at(up_outs, q)[...] = at(sels, q)[...] + at(up_ins, q)[...]
                up_copy(q).start()

    def downward(q, cond):
        @pl.when(jnp.logical_and(cond, has_down))
        def _():
            dn_copy(q).wait_recv()

            @pl.when(has_up)
            def _():
                at(dn_outs, q)[...] = at(sels, q)[...] + at(dn_ins, q)[...]
                dn_copy(q).start()

    def nearer(q):
        upward(q, lower)
        downward(q, jnp.logical_not(lower))

    def farther(q):
        downward(q, lower)
        upward(q, jnp.logical_not(lower))

    pair = (col, partner)
    if far is None:
        local[0].wait()
        taps_copy.wait_recv()
        edges_in(pair)
        for p in range(1, parts):
            for i, other in enumerate(order):
                image(p, i, other)
        for q in range(3):
            w_start(q)
        for p in range(parts):
            mine_in(p)
            convolve(p, pair)

            def other_chip(i, _):
                other = lax.rem(chip + i, n_chip)
                for who in (other * CORES, other * CORES + 1):
                    strip_in(p, who)
                    if p == 0:
                        edge_in(who)
                convolve(p, (other * CORES, other * CORES + 1))
                return 0

            lax.fori_loop(1, n_chip, other_chip, 0)
            if p == 0:
                for copy in local[3:]:
                    copy.wait()
            finish(p)
            select(p)
            if p == parts - 2:
                for q in range(TILES):
                    nearer(q)
    else:
        early = (near[0] * CORES, near[1] * CORES + 1)
        late = (near[0] * CORES + 1, near[1] * CORES)
        last = (far * CORES, far * CORES + 1)

        def relay_early(p):
            for k in range(2):
                strip_in(p, early[k])
                relay(p, k, early[k], near[1 - k])
                if p == 0:
                    edge_in(early[k])
                    on_my_edge(lambda to_core: edge_relay(k, early[k], near[1 - k])(to_core).start())

        for p in range(parts):
            if p + 1 < parts:
                image(p + 1, 0, order[0])
            if p < parts - 1:
                relay_early(p)
            if p + 1 < parts:
                image(p + 1, 1, order[1])
        local[0].wait()
        taps_copy.wait_recv()
        edges_in(pair)
        for p in range(parts):
            mine_in(p)
            convolve(p, pair + early)
            if p == parts - 2:
                relay_early(parts - 1)
                for q in range(3):
                    w_start(q)
            for group_of in (late, last):
                for who in group_of:
                    strip_in(p, who)
                    if p == 0:
                        edge_in(who)
                convolve(p, group_of)
            if p == 0:
                for copy in local[3:]:
                    copy.wait()
            if p == parts - 1:
                nearer(0)
                nearer(1)
            finish(p)
            select(p)

    for i in range(1, n_col):
        who = lax.rem(col + i, n_col)
        go(remote(hid.at[who], own.at[core, chip], asend.at[i], arecv.at[col], (row, who)))
    own[core, chip] = hid[col]

    others = near if far is None else [far] + near

    def tok_at(q, of_chip):
        return toks[q // TILES].at[of_chip, q % TILES]

    def t_start(q):
        for i, other in enumerate(others):
            go(remote(
                tok_at(q, chip), tok_at(q, chip), tsend.at[q, i], trecv.at[q, chip], (row, other * CORES + core)
            ))

    def t_wait(q):
        for other in others:
            remote(
                tok_at(q, chip), tok_at(q, other), tsend.at[q, 0], trecv.at[q, other], (row, partner)
            ).wait_recv()

    for q in range(2, TILES):
        nearer(q)
    w_near(0)
    w_near(1)
    w_near(2)
    query_copy = remote(queries.at[0], queries.at[1], qsend, qrecv, (row, partner))

    def weights(q):
        return wbuf[q].reshape(chans, chans)

    def ask():
        for i in range(1, n_col):
            who = lax.rem(col + i, n_col)
            remote(
                hid.at[0], own.at[lax.rem(who, CORES), who // CORES], asend.at[i], arecv.at[who], (row, partner)
            ).wait_recv()
        local[2].wait()
        for q in range(3):
            w_settle(q)

        mine = jnp.concatenate(
            [jnp.concatenate([own[c, k] for k in range(n_chip)], axis=1) for c in range(CORES)], axis=0
        )

        query = lax.dot_general(mine, weights(0), NT, preferred_element_type=jnp.float32).astype(jnp.bfloat16)
        query = jnp.dot(query, weights(1), preferred_element_type=jnp.float32)
        queries[0] = (query * chans ** (-0.5)).astype(jnp.bfloat16)
        query_copy.start()

    for q in range(slots):
        if q + TILES < slots:
            nearer(q + TILES)
        farther(q)
        tok_at(q, chip)[...] = at(sels, q)[...] + at(up_ins, q)[...] + at(dn_ins, q)[...]
        t_start(q)
        if q == slots - 5:
            for k in range(3):
                w_far(k)
        if q == slots - 2:
            ask()
    query_copy.wait_recv()

    def keys_of(q):
        found = toks[q // TILES]
        size = TILE_DEV * found.shape[3]
        return jnp.concatenate([found[k, q % TILES].reshape(size, group) for k in range(n_chip)], axis=1)

    def attend(query, keys, state):
        score = lax.dot_general(query, keys, NT, preferred_element_type=jnp.float32)
        fresh = jnp.max(score, axis=1, keepdims=True)
        if state is not None:
            fresh = jnp.maximum(fresh, state[0])
        weight = jnp.exp(score - fresh)
        total = jnp.sum(weight, axis=1, keepdims=True)
        accum = jnp.dot(weight.astype(jnp.bfloat16), keys, preferred_element_type=jnp.float32)
        if state is not None:
            factor = jnp.exp(state[0] - fresh)
            total = total + state[1] * factor
            accum = accum + state[2] * factor
        return fresh, total, accum

    steps = [range(t, t + TILES) for t in range(0, slots - TILES, TILES)]
    steps += [range(t, t + TILES // 2) for t in (slots - TILES, slots - TILES // 2)]
    states = [None, None]
    for t, step in enumerate(steps):
        for q in step:
            t_wait(q)
        keys = jnp.concatenate([keys_of(q) for q in step], axis=0)
        states[1] = attend(queries[1], keys, states[1])
        if t == len(steps) - 1:
            peak, total, accum = states[1]
            share_out[...] = (accum / total).astype(share_out.dtype)
            level_out[...] = jnp.broadcast_to(peak + jnp.log(total), level_out.shape)
            share_copies = [
                remote(share_out, share_in, ssend.at[0], srecv.at[0], (row, partner)),
                remote(level_out, level_in, ssend.at[1], srecv.at[1], (row, partner)),
            ]
            for copy in share_copies:
                copy.start()
        states[0] = attend(queries[0], keys, states[0])
    peak, total, accum = states[0]
    level, context = peak + jnp.log(total), accum / total
    for copy in share_copies:
        copy.wait_recv()
    keep = 1.0 / (1.0 + jnp.exp(level_in[:, :1] - level))
    context = context * keep + share_in[...].astype(jnp.float32) * (1.0 - keep)
    context = context.astype(jnp.bfloat16)
    attended = lax.dot_general(context, weights(2), NT, preferred_element_type=jnp.float32)
    local[1].wait()
    out_ref[...] = (lat[...].astype(jnp.float32) + attended.reshape(rows, cols, chans)).astype(out_ref.dtype)

    for to_core in range(CORES):

        @pl.when(core == 1 - to_core)
        def _():
            for p in range(parts):
                to_partner(p, to_core).wait_send()

    taps_copy.wait_send()
    query_copy.wait_send()
    for copy in share_copies:
        copy.wait_send()

    def edge_sent(to_core):
        for i in range(len(near)):
            edge_out(to_core, i).wait_send()

        @pl.when(core != to_core)
        def _():
            edge_out(to_core, len(near)).wait_send()

    on_edges(edge_sent)
    if far is not None:
        for p in range(parts):
            for k in range(2):
                relayed(p, k, early[k])
        for k in range(2):
            on_my_edge(lambda to_core: edge_relay(k, early[k], near[1 - k])(to_core).wait_send())

    @pl.when(has_down)
    def _():
        z_copy(0).wait_send()
        for q in range(slots):
            up_copy(q).wait_send()

    @pl.when(has_up)
    def _():
        z_copy(1).wait_send()
        for q in range(slots):
            dn_copy(q).wait_send()

    for copy in sends:
        copy.wait_send()


def vmem():
    return pl.BlockSpec(memory_space=pltpu.VMEM)


def anywhere():
    return pl.BlockSpec(memory_space=pl.ANY)


def body(n_row, n_col, latents, w_conv, conv_bias, w_qkv, owners):
    rows, cols, chans = latents.shape
    width = w_conv.shape[3]
    n_chip = n_col // CORES
    group, half = width * CORES, rows // CORES
    first = half // 4 * 2 + 2
    spans = (first, half - first)
    count, slots, parts = half * cols, len(spans) * TILES, len(spans)
    dma = pltpu.SemaphoreType.DMA
    bf16 = jnp.bfloat16
    line = tuple(pltpu.VMEM((TILES, TILE_DEV, span * cols, group), bf16) for span in spans)
    tokens = tuple(pltpu.VMEM((n_chip, TILES, TILE_DEV, span * cols, group), bf16) for span in spans)
    return pl.pallas_call(
        functools.partial(block_kernel, n_row, n_col, spans),
        out_shape=pltpu.VMEM((rows, cols, chans), bf16),
        in_specs=[anywhere()] * 5,
        out_specs=vmem(),
        scratch_shapes=[
            pltpu.SMEM((TILES,), jnp.int32),
            pltpu.VMEM((1, chans), jnp.float32),
            pltpu.VMEM((n_col, half + 2, cols, chans), bf16),
            pltpu.VMEM((rows, cols, chans), bf16),
            pltpu.VMEM((2, cols, chans), bf16),
            pltpu.VMEM((3, 3, CORES, width, chans), bf16),
            pltpu.VMEM((n_col, half, cols, 3 * group), jnp.float32),
            pltpu.VMEM((n_col, count, group), bf16),
            line, line, line, line, line, tokens,
            pltpu.VMEM((CORES, n_chip, count, group), bf16),
            pltpu.VMEM((3, n_col, width, chans), bf16),
            pltpu.VMEM((CORES, rows * cols, chans), bf16),
            pltpu.VMEM((rows * cols, chans), bf16),
            pltpu.VMEM((rows * cols, chans), bf16),
            pltpu.VMEM((rows * cols, 128), jnp.float32),
            pltpu.VMEM((rows * cols, 128), jnp.float32),
            dma((6 + parts,)), dma((parts, max(n_chip - 1, 3), CORES)), dma((parts, n_col)),
            dma((2,)), dma((2,)), dma((2, n_chip)), dma((n_col,)), dma((3 + parts,)), dma,
            dma((slots,)), dma((slots,)), dma((slots,)), dma((slots,)),
            dma((slots, n_chip)), dma((slots, n_chip)), dma, dma, dma((2,)), dma((2,)),
            dma((n_col,)), dma((n_col,)),
            dma((3, n_chip)), dma((3, n_col)), dma((3, n_chip)),
        ],
        compiler_params=pltpu.CompilerParams(
            collective_id=0, has_side_effects=True, vmem_limit_bytes=VMEM_LIMIT
        ),
    )(
        owners, latents, jnp.transpose(w_conv, (0, 1, 3, 2)), conv_bias.reshape(1, chans),
        jnp.transpose(w_qkv, (0, 2, 1)),
    )


def solution(mesh):
    placed = (P("row", "col", None), P(None, None, None, "col"), P(), P(None, None, "col"), P())
    return jax.shard_map(
        functools.partial(body, mesh.shape["row"], mesh.shape["col"]),
        mesh=mesh, in_specs=placed, out_specs=P("row", "col", None), check_vma=False,
    )
```

```python
import functools

import jax
import jax.numpy as jnp
from jax import lax
from jax.experimental import pallas as pl
from jax.experimental.pallas import tpu as pltpu
from jax.sharding import PartitionSpec as P

TILES = 4
TILE_DEV = 2
CORES = 2
MESH = pl.DeviceIdType.MESH
VMEM_LIMIT = 56 * 1024 * 1024
NT = (((1,), (1,)), ((), ()))


def remote(src, dst, send, recv, target):
    return pltpu.make_async_remote_copy(
        src_ref=src, dst_ref=dst, send_sem=send, recv_sem=recv, device_id=target, device_id_type=MESH
    )


def chips_around(chip, n_chip):
    if n_chip == 4:
        beside = chip + 1 - 2 * lax.rem(chip, 2)
        across = lax.rem(chip + 2, n_chip)
        return [beside, across], lax.rem(beside + 2, n_chip)
    return [lax.rem(chip + i, n_chip) for i in range(1, n_chip)], None


def spread(row, col, n_col, src, place, send, recv, fsend, sends):
    chip, core = col // CORES, lax.rem(col, CORES)
    n_chip = n_col // CORES
    partner = chip * CORES + 1 - core
    near, far = chips_around(chip, n_chip)

    def go(source, target, send_sem, recv_sem, device):
        copy = remote(source, target, send_sem, recv_sem, (row, device))
        copy.start()
        sends.append(copy)

    def start(q):
        for i, other in enumerate(near if q % 2 == 0 else near[::-1]):
            go(src(q), place(q, col), send.at[q, i], recv.at[q, col], other * CORES + core)
        go(src(q), place(q, col), fsend.at[q, chip], recv.at[q, col], partner)

    def wait(q, who):
        remote(src(q), place(q, who), fsend.at[q, chip], recv.at[q, who], (row, partner)).wait_recv()

    def forward(q, origin):
        who = origin * CORES + core
        go(place(q, who), place(q, who), fsend.at[q, origin], recv.at[q, who], partner)

    def pass_near(q):
        order = near if q % 2 == 0 else near[::-1]
        for k, origin in enumerate(order):
            who = origin * CORES + core
            wait(q, who)
            if far is not None and k == 0:
                go(place(q, who), place(q, who), send.at[q, 2], recv.at[q, who], order[1] * CORES + core)
            forward(q, origin)

    def pass_far(q):
        if far is not None:
            wait(q, far * CORES + core)
            forward(q, far)

    def settle(q):
        for i in range(n_chip):
            wait(q, lax.rem(chip + i, n_chip) * CORES + 1 - core)

    return start, pass_near, pass_far, settle


def block_kernel(
    n_row, n_col, spans, owners_hbm, lat_ref, taps_ref, bias_hbm, w_ref, out_ref,
    owners_ref, bias_ref, img, lat, edges, taps, wide, hid,
    sels, up_ins, up_outs, dn_ins, dn_outs, toks, own, wbuf, queries, share_out, share_in, level_out, level_in,
    lsem, isend, irecv, zsend, zrecv, hsend, hrecv, csend, crecv,
    up_send, up_recv, dn_send, dn_recv, tsend, trecv, qsend, qrecv, ssend, srecv,
    asend, arecv, wsend, wrecv, wfsend,
):
    row, col = lax.axis_index("row"), lax.axis_index("col")
    chip, core = col // CORES, lax.rem(col, CORES)
    n_chip = n_col // CORES
    partner = chip * CORES + 1 - core
    near, far = chips_around(chip, n_chip)
    rows, cols, chans = lat_ref.shape
    half = rows // CORES
    group = hid.shape[2]
    count = half * cols
    parts = len(spans)
    starts = [sum(spans[:p]) for p in range(parts)]
    slots = parts * TILES
    has_up, has_down = row > 0, row < n_row - 1
    top = core == 0

    barrier = pltpu.get_barrier_semaphore()

    def hello(target):
        pl.semaphore_signal(barrier, inc=1, device_id=target, device_id_type=MESH)

    @pl.when(has_up)
    def _():
        hello((row - 1, col))

    @pl.when(has_down)
    def _():
        hello((row + 1, col))

    for other in near:
        for c in range(CORES):
            hello((row, other * CORES + c))
    hello((row, partner))

    inner = tuple(start + 2 for start in starts[1:])
    own_rows = ((1, *inner, half + 2), (0, *inner, half + 1))

    def piece(p, to_core, who=None):
        lo, hi = own_rows[to_core][p], own_rows[to_core][p + 1]
        if who is None:
            return lat_ref.at[pl.ds(lo - 1 + to_core * half, hi - lo)]
        return img.at[who, pl.ds(lo, hi - lo)]

    local = [
        pltpu.make_async_copy(taps_ref, taps.at[:, :, core], lsem.at[0]),
        pltpu.make_async_copy(lat_ref, lat, lsem.at[1]),
        pltpu.make_async_copy(w_ref, wbuf.at[:, col], lsem.at[2]),
        pltpu.make_async_copy(bias_hbm, bias_ref, lsem.at[3]),
        pltpu.make_async_copy(owners_hbm, owners_ref, lsem.at[4]),
    ]

    def edge_row(to_core):
        return 0 if to_core == 0 else half + 1

    @pl.when(jnp.logical_and(top, jnp.logical_not(has_up)))
    def _():
        for who in range(n_col):
            img[who, edge_row(0)] = jnp.zeros((cols, chans), img.dtype)

    @pl.when(jnp.logical_and(jnp.logical_not(top), jnp.logical_not(has_down)))
    def _():
        for who in range(n_col):
            img[who, edge_row(1)] = jnp.zeros((cols, chans), img.dtype)

    pl.semaphore_wait(barrier, CORES * len(near) + 1 + has_up.astype(jnp.int32) + has_down.astype(jnp.int32))

    sends = []

    def go(copy):
        copy.start()
        sends.append(copy)

    def z_copy(to_core):
        if to_core == 0:
            return remote(lat_ref.at[rows - 1], edges.at[0], zsend.at[0], zrecv.at[0], (row + 1, col))
        return remote(lat_ref.at[0], edges.at[1], zsend.at[1], zrecv.at[1], (row - 1, col))

    @pl.when(has_down)
    def _():
        z_copy(0).start()

    @pl.when(has_up)
    def _():
        z_copy(1).start()

    def image(p, i, other):
        for to_core in range(CORES):
            go(remote(
                piece(p, to_core), piece(p, to_core, col), isend.at[p, i, to_core], irecv.at[p, col],
                (row, other * CORES + to_core),
            ))

    if far is None:
        order = near
    else:
        order = [jnp.where(top, near[0], near[1]), jnp.where(top, near[1], near[0])]
    for i, other in enumerate(order):
        image(0, i, other)

    taps_copy = remote(taps_ref, taps.at[:, :, core], csend.at[0], crecv, (row, partner))
    taps_copy.start()
    local[0].start()

    def to_partner(p, to_core):
        return remote(
            piece(p, to_core), piece(p, to_core, col), csend.at[3 + p], irecv.at[p, col], (row, chip * CORES + to_core)
        )

    def to_self(p, to_core):
        return pltpu.make_async_copy(piece(p, to_core), piece(p, to_core, col), lsem.at[6 + p])

    for to_core in range(CORES):

        @pl.when(core == to_core)
        def _():
            for p in range(parts):
                to_self(p, to_core).start()

        @pl.when(core == 1 - to_core)
        def _():
            for p in range(parts):
                to_partner(p, to_core).start()

    for copy in local[1:]:
        copy.start()

    def edge_place(to_core, who):
        return img.at[who, edge_row(to_core)]

    def edge_out(to_core, i):
        if i < len(near):
            target = near[i] * CORES + to_core
        else:
            target = partner
        return remote(
            edges.at[to_core], edge_place(to_core, col), hsend.at[to_core, i], hrecv.at[col], (row, target)
        )

    def edge_self(to_core):
        return pltpu.make_async_copy(edges.at[to_core], edge_place(to_core, col), lsem.at[5])

    def on_edges(act):
        for to_core in range(CORES):

            @pl.when(has_up if to_core == 0 else has_down)
            def _():
                act(to_core)

    def edge_spread(to_core):
        z_copy(to_core).wait_recv()
        for i in range(len(near)):
            edge_out(to_core, i).start()

        @pl.when(core == to_core)
        def _():
            edge_self(to_core).start()

        @pl.when(core != to_core)
        def _():
            edge_out(to_core, len(near)).start()

    on_edges(edge_spread)

    def on_my_edge(act):
        for to_core in range(CORES):

            @pl.when(jnp.logical_and(core == to_core, has_up if to_core == 0 else has_down))
            def _():
                act(to_core)

    def edge_in(who):
        on_my_edge(lambda to_core: remote(
            edges.at[to_core], edge_place(to_core, who), csend.at[0], hrecv.at[who], (row, partner)
        ).wait_recv())

    def strip_in(p, who):
        for to_core in range(CORES):

            @pl.when(core == to_core)
            def _():
                remote(
                    piece(p, to_core, who), piece(p, to_core, who), csend.at[0], irecv.at[p, who], (row, partner)
                ).wait_recv()

    def relay(p, k, who, target):
        for to_core in range(CORES):

            @pl.when(core == to_core)
            def _():
                remote(
                    piece(p, to_core, who), piece(p, to_core, who), isend.at[p, 2, k], irecv.at[p, who],
                    (row, target * CORES + to_core),
                ).start()

    def relayed(p, k, who):
        for to_core in range(CORES):

            @pl.when(core == to_core)
            def _():
                remote(
                    piece(p, to_core, who), piece(p, to_core, who), isend.at[p, 2, k], irecv.at[p, who],
                    (row, partner),
                ).wait_send()

    def edge_relay(k, who, target):
        return lambda to_core: remote(
            edge_place(to_core, who), edge_place(to_core, who), csend.at[1 + k], hrecv.at[who],
            (row, target * CORES + to_core),
        )

    def convolve(p, group_of):
        size = spans[p] * cols
        total = None
        for tap in range(3):
            window = jnp.concatenate(
                [img[who, pl.ds(starts[p] + tap, spans[p])].reshape(size, chans) for who in group_of], axis=0
            )
            kernel = taps[tap].reshape(3 * group, chans)
            part = lax.dot_general(window, kernel, NT, preferred_element_type=jnp.float32)
            total = part if total is None else total + part
        for i, who in enumerate(group_of):
            wide[who, pl.ds(starts[p], spans[p])] = total[i * size:(i + 1) * size].reshape(
                spans[p], cols, 3 * group
            )

    def finish(p):
        bias = None
        for k in range(n_chip):
            mine = jnp.where(chip == k, bias_ref[:, k * group:(k + 1) * group], 0.0)
            bias = mine if bias is None else bias + mine
        bias = bias.reshape(1, 1, group)
        shape = (spans[p], cols, group)
        at = lax.broadcasted_iota(jnp.int32, shape, 1)

        def part_of(who, tap):
            return wide[who, pl.ds(starts[p], spans[p]), :, pl.ds(tap * group, group)]

        previous = jnp.zeros(shape, jnp.float32)
        after = pltpu.roll(part_of(0, 2), cols - 1, 1)
        for who in range(n_col):
            left = pltpu.roll(part_of(who, 0), 1, 1)
            right = after
            if who + 1 < n_col:
                after = pltpu.roll(part_of(who + 1, 2), cols - 1, 1)
            else:
                after = jnp.zeros(shape, jnp.float32)
            conv = part_of(who, 1) + jnp.where(at == 0, previous, left) + jnp.where(at == cols - 1, after, right)
            previous = left
            conv = (conv + bias).reshape(spans[p] * cols, group)
            hid[who, pl.ds(starts[p] * cols, spans[p] * cols)] = (conv * jax.nn.sigmoid(conv)).astype(hid.dtype)

    def at(pair, q):
        return pair[q // TILES].at[q % TILES]

    def up_copy(q):
        return remote(at(up_outs, q), at(up_ins, q), up_send.at[q], up_recv.at[q], (row + 1, col))

    def dn_copy(q):
        return remote(at(dn_outs, q), at(dn_ins, q), dn_send.at[q], dn_recv.at[q], (row - 1, col))

    def select(p):
        for tile in range(TILES):
            q = p * TILES + tile
            flat = TILE_DEV * owners_ref[tile]
            here = flat // n_col == row
            for member in range(TILE_DEV):
                block = hid[lax.rem(flat, n_col) + member, pl.ds(starts[p] * cols, spans[p] * cols)]
                block = jnp.where(here, block, jnp.zeros_like(block))
                at(sels, q)[member] = block

            @pl.when(jnp.logical_not(has_up))
            def _():
                at(up_outs, q)[...] = at(sels, q)[...]
                up_copy(q).start()
                at(up_ins, q)[...] = jnp.zeros(up_ins[p].shape[1:], hid.dtype)

            @pl.when(jnp.logical_not(has_down))
            def _():
                at(dn_outs, q)[...] = at(sels, q)[...]
                dn_copy(q).start()
                at(dn_ins, q)[...] = jnp.zeros(dn_ins[p].shape[1:], hid.dtype)

    w_start, w_near, w_far, w_settle = spread(
        row, col, n_col, lambda q: w_ref.at[q], lambda q, who: wbuf.at[q, who],
        wsend, wrecv, wfsend, sends,
    )

    def mine_in(p):
        for to_core in range(CORES):

            @pl.when(core == to_core)
            def _():
                to_self(p, to_core).wait()

        strip_in(p, partner)

    def edges_in(group_of):
        for who in group_of:
            if who is col:
                on_my_edge(lambda to_core: edge_self(to_core).wait())
            else:
                edge_in(who)

    lower = row < n_row // 2

    def upward(q, cond):
        @pl.when(jnp.logical_and(cond, has_up))
        def _():
            up_copy(q).wait_recv()

            @pl.when(has_down)
            def _():
                at(up_outs, q)[...] = at(sels, q)[...] + at(up_ins, q)[...]
                up_copy(q).start()

    def downward(q, cond):
        @pl.when(jnp.logical_and(cond, has_down))
        def _():
            dn_copy(q).wait_recv()

            @pl.when(has_up)
            def _():
                at(dn_outs, q)[...] = at(sels, q)[...] + at(dn_ins, q)[...]
                dn_copy(q).start()

    def nearer(q):
        upward(q, lower)
        downward(q, jnp.logical_not(lower))

    def farther(q):
        downward(q, lower)
        upward(q, jnp.logical_not(lower))

    pair = (col, partner)
    if far is None:
        local[0].wait()
        taps_copy.wait_recv()
        edges_in(pair)
        for p in range(1, parts):
            for i, other in enumerate(order):
                image(p, i, other)
        for q in range(3):
            w_start(q)
        for p in range(parts):
            mine_in(p)
            convolve(p, pair)

            def other_chip(i, _):
                other = lax.rem(chip + i, n_chip)
                for who in (other * CORES, other * CORES + 1):
                    strip_in(p, who)
                    if p == 0:
                        edge_in(who)
                convolve(p, (other * CORES, other * CORES + 1))
                return 0

            lax.fori_loop(1, n_chip, other_chip, 0)
            if p == 0:
                for copy in local[3:]:
                    copy.wait()
            finish(p)
            select(p)
            if p == parts - 2:
                for q in range(TILES):
                    nearer(q)
    else:
        early = (near[0] * CORES, near[1] * CORES + 1)
        late = (near[0] * CORES + 1, near[1] * CORES)
        last = (far * CORES, far * CORES + 1)

        def relay_early(p):
            for k in range(2):
                strip_in(p, early[k])
                relay(p, k, early[k], near[1 - k])
                if p == 0:
                    edge_in(early[k])
                    on_my_edge(lambda to_core: edge_relay(k, early[k], near[1 - k])(to_core).start())

        for p in range(parts):
            if p + 1 < parts:
                image(p + 1, 0, order[0])
            if p < parts - 1:
                relay_early(p)
            if p + 1 < parts:
                image(p + 1, 1, order[1])
        local[0].wait()
        taps_copy.wait_recv()
        edges_in(pair)
        for p in range(parts):
            mine_in(p)
            convolve(p, pair + early)
            if p == parts - 2:
                relay_early(parts - 1)
                for q in range(3):
                    w_start(q)
            for group_of in (late, last):
                for who in group_of:
                    strip_in(p, who)
                    if p == 0:
                        edge_in(who)
                convolve(p, group_of)
            if p == 0:
                for copy in local[3:]:
                    copy.wait()
            if p == parts - 1:
                nearer(0)
                nearer(1)
            finish(p)
            select(p)

    for i in range(1, n_col):
        who = lax.rem(col + i, n_col)
        go(remote(hid.at[who], own.at[core, chip], asend.at[i], arecv.at[col], (row, who)))
    own[core, chip] = hid[col]

    others = near if far is None else [far] + near

    def tok_at(q, of_chip):
        return toks[q // TILES].at[of_chip, q % TILES]

    def t_start(q):
        for i, other in enumerate(others if q >= TILES else others[::-1]):
            go(remote(
                tok_at(q, chip), tok_at(q, chip), tsend.at[q, i], trecv.at[q, chip], (row, other * CORES + core)
            ))

    def t_wait(q):
        for other in others:
            remote(
                tok_at(q, chip), tok_at(q, other), tsend.at[q, 0], trecv.at[q, other], (row, partner)
            ).wait_recv()

    for q in range(2, TILES):
        nearer(q)
    w_near(0)
    w_near(1)
    w_near(2)
    query_copy = remote(queries.at[0], queries.at[1], qsend, qrecv, (row, partner))

    def weights(q):
        return wbuf[q].reshape(chans, chans)

    def ask():
        for i in range(1, n_col):
            who = lax.rem(col + i, n_col)
            remote(
                hid.at[0], own.at[lax.rem(who, CORES), who // CORES], asend.at[i], arecv.at[who], (row, partner)
            ).wait_recv()
        local[2].wait()
        for q in range(3):
            w_settle(q)

        mine = jnp.concatenate(
            [jnp.concatenate([own[c, k] for k in range(n_chip)], axis=1) for c in range(CORES)], axis=0
        )

        query = lax.dot_general(mine, weights(0), NT, preferred_element_type=jnp.float32).astype(jnp.bfloat16)
        query = jnp.dot(query, weights(1), preferred_element_type=jnp.float32)
        queries[0] = (query * chans ** (-0.5)).astype(jnp.bfloat16)
        query_copy.start()

    for q in range(slots):
        if q + TILES < slots:
            nearer(q + TILES)
        farther(q)
        tok_at(q, chip)[...] = at(sels, q)[...] + at(up_ins, q)[...] + at(dn_ins, q)[...]
        t_start(q)
        if q == slots - 5:
            for k in range(3):
                w_far(k)
        if q == slots - 2:
            ask()
    query_copy.wait_recv()

    def keys_of(q):
        found = toks[q // TILES]
        size = TILE_DEV * found.shape[3]
        return jnp.concatenate([found[k, q % TILES].reshape(size, group) for k in range(n_chip)], axis=1)

    def attend(query, keys, state):
        score = lax.dot_general(query, keys, NT, preferred_element_type=jnp.float32)
        fresh = jnp.max(score, axis=1, keepdims=True)
        if state is not None:
            fresh = jnp.maximum(fresh, state[0])
        weight = jnp.exp(score - fresh)
        total = jnp.sum(weight, axis=1, keepdims=True)
        accum = jnp.dot(weight.astype(jnp.bfloat16), keys, preferred_element_type=jnp.float32)
        if state is not None:
            factor = jnp.exp(state[0] - fresh)
            total = total + state[1] * factor
            accum = accum + state[2] * factor
        return fresh, total, accum

    steps = [range(t, t + TILES) for t in range(0, slots - TILES, TILES)]
    steps += [range(t, t + TILES // 2) for t in (slots - TILES, slots - TILES // 2)]
    states = [None, None]
    for t, step in enumerate(steps):
        for q in step:
            t_wait(q)
        keys = jnp.concatenate([keys_of(q) for q in step], axis=0)
        states[1] = attend(queries[1], keys, states[1])
        if t == len(steps) - 1:
            peak, total, accum = states[1]
            share_out[...] = (accum / total).astype(share_out.dtype)
            level_out[...] = jnp.broadcast_to(peak + jnp.log(total), level_out.shape)
            share_copies = [
                remote(share_out, share_in, ssend.at[0], srecv.at[0], (row, partner)),
                remote(level_out, level_in, ssend.at[1], srecv.at[1], (row, partner)),
            ]
            for copy in share_copies:
                copy.start()
        states[0] = attend(queries[0], keys, states[0])
    peak, total, accum = states[0]
    level, context = peak + jnp.log(total), accum / total
    for copy in share_copies:
        copy.wait_recv()
    keep = 1.0 / (1.0 + jnp.exp(level_in[:, :1] - level))
    context = context * keep + share_in[...].astype(jnp.float32) * (1.0 - keep)
    context = context.astype(jnp.bfloat16)
    attended = lax.dot_general(context, weights(2), NT, preferred_element_type=jnp.float32)
    local[1].wait()
    out_ref[...] = (lat[...].astype(jnp.float32) + attended.reshape(rows, cols, chans)).astype(out_ref.dtype)

    for to_core in range(CORES):

        @pl.when(core == 1 - to_core)
        def _():
            for p in range(parts):
                to_partner(p, to_core).wait_send()

    taps_copy.wait_send()
    query_copy.wait_send()
    for copy in share_copies:
        copy.wait_send()

    def edge_sent(to_core):
        for i in range(len(near)):
            edge_out(to_core, i).wait_send()

        @pl.when(core != to_core)
        def _():
            edge_out(to_core, len(near)).wait_send()

    on_edges(edge_sent)
    if far is not None:
        for p in range(parts):
            for k in range(2):
                relayed(p, k, early[k])
        for k in range(2):
            on_my_edge(lambda to_core: edge_relay(k, early[k], near[1 - k])(to_core).wait_send())

    @pl.when(has_down)
    def _():
        z_copy(0).wait_send()
        for q in range(slots):
            up_copy(q).wait_send()

    @pl.when(has_up)
    def _():
        z_copy(1).wait_send()
        for q in range(slots):
            dn_copy(q).wait_send()

    for copy in sends:
        copy.wait_send()


def vmem():
    return pl.BlockSpec(memory_space=pltpu.VMEM)


def anywhere():
    return pl.BlockSpec(memory_space=pl.ANY)


def body(n_row, n_col, latents, w_conv, conv_bias, w_qkv, owners):
    rows, cols, chans = latents.shape
    width = w_conv.shape[3]
    n_chip = n_col // CORES
    group, half = width * CORES, rows // CORES
    first = half // 4 * 2 + 2
    spans = (first, half - first)
    count, slots, parts = half * cols, len(spans) * TILES, len(spans)
    dma = pltpu.SemaphoreType.DMA
    bf16 = jnp.bfloat16
    line = tuple(pltpu.VMEM((TILES, TILE_DEV, span * cols, group), bf16) for span in spans)
    tokens = tuple(pltpu.VMEM((n_chip, TILES, TILE_DEV, span * cols, group), bf16) for span in spans)
    return pl.pallas_call(
        functools.partial(block_kernel, n_row, n_col, spans),
        out_shape=pltpu.VMEM((rows, cols, chans), bf16),
        in_specs=[anywhere()] * 5,
        out_specs=vmem(),
        scratch_shapes=[
            pltpu.SMEM((TILES,), jnp.int32),
            pltpu.VMEM((1, chans), jnp.float32),
            pltpu.VMEM((n_col, half + 2, cols, chans), bf16),
            pltpu.VMEM((rows, cols, chans), bf16),
            pltpu.VMEM((2, cols, chans), bf16),
            pltpu.VMEM((3, 3, CORES, width, chans), bf16),
            pltpu.VMEM((n_col, half, cols, 3 * group), jnp.float32),
            pltpu.VMEM((n_col, count, group), bf16),
            line, line, line, line, line, tokens,
            pltpu.VMEM((CORES, n_chip, count, group), bf16),
            pltpu.VMEM((3, n_col, width, chans), bf16),
            pltpu.VMEM((CORES, rows * cols, chans), bf16),
            pltpu.VMEM((rows * cols, chans), bf16),
            pltpu.VMEM((rows * cols, chans), bf16),
            pltpu.VMEM((rows * cols, 128), jnp.float32),
            pltpu.VMEM((rows * cols, 128), jnp.float32),
            dma((6 + parts,)), dma((parts, max(n_chip - 1, 3), CORES)), dma((parts, n_col)),
            dma((2,)), dma((2,)), dma((2, n_chip)), dma((n_col,)), dma((3 + parts,)), dma,
            dma((slots,)), dma((slots,)), dma((slots,)), dma((slots,)),
            dma((slots, n_chip)), dma((slots, n_chip)), dma, dma, dma((2,)), dma((2,)),
            dma((n_col,)), dma((n_col,)),
            dma((3, n_chip)), dma((3, n_col)), dma((3, n_chip)),
        ],
        compiler_params=pltpu.CompilerParams(
            collective_id=0, has_side_effects=True, vmem_limit_bytes=VMEM_LIMIT
        ),
    )(
        owners, latents, jnp.transpose(w_conv, (0, 1, 3, 2)), conv_bias.reshape(1, chans),
        jnp.transpose(w_qkv, (0, 2, 1)),
    )


def solution(mesh):
    placed = (P("row", "col", None), P(None, None, None, "col"), P(), P(None, None, "col"), P())
    return jax.shard_map(
        functools.partial(body, mesh.shape["row"], mesh.shape["col"]),
        mesh=mesh, in_specs=placed, out_specs=P("row", "col", None), check_vma=False,
    )
```
